32 devices in a mesh: rep: 8 (over y, x, core), grp: 4 (over z).
Axes of the slice: x: 2, y: 2, z: 4, core: 2. Of those that a mesh axis runs over, the one named last changes fastest.
Arguments:
- tokens: bfloat16 [64, 512, 896], P(('rep', 'grp')), may hold values from -6 to 6
- doc_ids: int32 [64, 512], P(('rep', 'grp')), may hold values from 0 to 3, never falling along the last dimension, each value on 1 to 256 neighbouring positions
- neighbours: bfloat16 [1024, 128, 896], P(('rep', 'grp')), may hold values from -6 to 6
- neighbour_rows: int32 [512, 2], P(('rep', 'grp')), may hold values from 0 to 1023, as said below
- out_grad: bfloat16 [64, 512, 896], P(('rep', 'grp')), may hold values from -6 to 6
- attn_gain: bfloat16 [896], P('grp'), may hold values from 0.099609375 to 1.8984375
- attn_query: bfloat16 [896, 896], P('grp'), may hold values from -0.1875 to 0.1875
- attn_key: bfloat16 [896, 896], P('grp'), may hold values from -0.1875 to 0.1875
- attn_value: bfloat16 [896, 896], P('grp'), may hold values from -0.1875 to 0.1875
- bias_content: bfloat16 [896], P('grp'), may hold values from -3 to 3
- bias_position: bfloat16 [896], P('grp'), may hold values from -3 to 3
- rel_proj: bfloat16 [896, 896], P('grp'), may hold values from -0.1875 to 0.1875
- attn_proj: bfloat16 [896, 896], P('grp'), may hold values from -1 to 1
- cross_gain: bfloat16 [896], P('grp'), may hold values from 0.099609375 to 1.8984375
- cross_query: bfloat16 [896, 896], P('grp'), may hold values from -0.1875 to 0.1875
- cross_key: bfloat16 [896, 896], P('grp'), may hold values from -0.1875 to 0.1875
- cross_value: bfloat16 [896, 896], P('grp'), may hold values from -0.1875 to 0.1875
- cross_proj: bfloat16 [896, 896], P('grp'), may hold values from -1 to 1
- ffn_gain: bfloat16 [896], P('grp'), may hold values from 0.099609375 to 1.8984375
- ffn_up: bfloat16 [896, 3584], P('grp'), may hold values from -0.1875 to 0.1875
- ffn_down: bfloat16 [3584, 896], P('grp'), may hold values from -0.09375 to 0.09375
Outputs:
- mixed_out: bfloat16 [64, 512, 896], P(('rep', 'grp'))
- tokens_grad: bfloat16 [64, 512, 896], P(('rep', 'grp'))
- neighbours_grad: bfloat16 [1024, 128, 896], P(('rep', 'grp'))
- attn_gain_grad: float32 [896], P('grp')
- attn_query_grad: float32 [896, 896], P('grp')
- attn_key_grad: float32 [896, 896], P('grp')
- attn_value_grad: float32 [896, 896], P('grp')
- bias_content_grad: float32 [896], P('grp')
- bias_position_grad: float32 [896], P('grp')
- rel_proj_grad: float32 [896, 896], P('grp')
- attn_proj_grad: float32 [896, 896], P('grp')
- cross_gain_grad: float32 [896], P('grp')
- cross_query_grad: float32 [896, 896], P('grp')
- cross_key_grad: float32 [896, 896], P('grp')
- cross_value_grad: float32 [896, 896], P('grp')
- cross_proj_grad: float32 [896, 896], P('grp')
- ffn_gain_grad: float32 [896], P('grp')
- ffn_up_grad: float32 [896, 3584], P('grp')
- ffn_down_grad: float32 [3584, 896], P('grp')
The draws below stay inside these ranges and needn't reach their ends.
Inputs may be any that keep to these rules, and one draw needn't show every extreme that they name: `doc_ids`: along a sequence the document numbers never fall; a document has 1 to 256 tokens, and some document has exactly 256. `neighbour_rows`: the rows are laid out in blocks of 16 stretches, in the order of the sequences; the stretches of block b name each of the rows b * 2 * 512 // 64 * 2 to (b + 1) * 2 * 512 // 64 * 2 - 1 of neighbours exactly once.
All inputs are finite; a program needn't handle non-finite values.
Results may differ from the reference program's by a relative error of at most 0.028.
Values may be sent and summed in bfloat16 or wider, within the bound.
No kernel may reach another device: no remote copies, remote signals or barrier semaphores. Data moves between devices by JAX's collectives and lax.ppermute only.
A program may use at most 384 MiB of HBM per device.

```python
import math
import jax
import jax.numpy as jnp
import numpy as np
from jax import lax

D = 896
HEADS = 14
HDIM = 64
FF = 3584
STRETCH = 64
NEIGH = 2
NLEN = 128
BLOCK = 256
SEQ_LEN = 512
SEQ_DEV = 2
SEQS = 64
STRETCHES = 512
NB_ROWS = 1024


def draw_neighbour_rows(key, part):
    block = SEQ_DEV * (SEQ_LEN // STRETCH) * NEIGH
    count = NB_ROWS // block
    keys = jax.random.split(key, count)

    def one_order(single):
        return jax.random.permutation(single, block)
    orders = jax.vmap(one_order)(keys)
    offsets = jnp.arange(count, dtype=jnp.int32)[:, None] * block
    return (orders.astype(jnp.int32) + offsets).reshape(STRETCHES, NEIGH)


def shard_levels(stream_key, dims, pieces, least, largest):
    level = 1.0
    for position, parts in pieces:
        steps = jax.random.uniform(jax.random.fold_in(jax.random.fold_in(stream_key, 6), position), (parts,), jnp.float32, least / len(pieces), largest / len(pieces))
        level = level * jnp.repeat(jnp.exp(steps), dims[position] // parts).reshape((-1,) + (1,) * (len(dims) - 1 - position))
    return level


def split_up(count, total, most, skew):
    weights = [(1 << 20) // math.isqrt(grade ** skew) + 1 for grade in range(2, count + 1)]
    rest, counts = total - most - (count - 1), [1] * (count - 1)
    while rest > 0:
        free = [i for i in range(count - 1) if counts[i] < most]
        whole, budget = sum([weights[i] for i in free]), rest
        for i in free:
            more = min(most - counts[i], max(1, budget * weights[i] // whole), rest)
            counts[i] = counts[i] + more
            rest = rest - more
    return np.array([most] + counts)


def ragged_sizes(stream_key, amount, total, reach, skew):
    if amount == 2:
        one = jax.random.randint(stream_key, (), max(1, total - reach), min(reach, total - 1) + 1)
        return jnp.stack([one, total - one])
    tallies = jnp.asarray(split_up(amount, total, reach, skew), jnp.int32)
    couples = (amount - 1) // 2
    donor, receiver = tallies[1:1 + 2 * couples:2], tallies[2:2 + 2 * couples:2]
    margin = jnp.minimum(donor - 1, reach - receiver)
    moved = jax.random.randint(jax.random.fold_in(stream_key, 1), (couples,), 0, 1 << 20) % (margin + 1)
    tallies = tallies.at[1:1 + 2 * couples:2].set(donor - moved).at[2:2 + 2 * couples:2].set(receiver + moved)
    return tallies[jax.random.permutation(jax.random.fold_in(stream_key, 2), amount)]


def centred(rng, shape, scale, most, shards=(), kind=jnp.bfloat16):
    loudness = shard_levels(rng, shape, shards, -0.22, 0.18) if shards else 1.0
    values = jax.random.normal(rng, shape, jnp.float32) * scale * loudness
    return jnp.minimum(jnp.maximum(values, -most), most).astype(kind)


def setup_inputs(seed: int = 0) -> dict:
    key_of = jax.random.split(jax.random.key(seed), 22)
    return {
        "tokens": centred(key_of[0], (SEQS, SEQ_LEN, D), 1.0, 6.0, ((0, 32),)),
        "doc_ids": jax.vmap(lambda own: jnp.searchsorted(jnp.cumsum(ragged_sizes(own, 4, SEQ_LEN, SEQ_LEN // 2, 2)), jnp.arange(SEQ_LEN), side="right"))(jax.random.split(key_of[1], SEQS)).reshape((SEQS, SEQ_LEN)).astype(jnp.int32),
        "neighbours": centred(key_of[2], (NB_ROWS, NLEN, D), 1.0, 6.0, ((0, 32),)),
        "neighbour_rows": draw_neighbour_rows(jax.random.fold_in(key_of[21], 71), 0),
        "out_grad": centred(key_of[4], (SEQS, SEQ_LEN, D), 1.0, 6.0, ((0, 32),)),
        "attn_gain": jnp.clip(1.0 + 0.18 * jax.random.normal(key_of[5], (D,), jnp.float32), 0.099609375, 1.8984375).astype(jnp.bfloat16),
        "attn_query": centred(key_of[6], (D, D), D ** -0.5, 0.1875, ((0, 4),)),
        "attn_key": centred(key_of[7], (D, D), D ** -0.5, 0.1875, ((0, 4),)),
        "attn_value": centred(key_of[8], (D, D), D ** -0.5, 0.1875, ((0, 4),)),
        "bias_content": centred(key_of[9], (D,), 0.5, 3.0, ((0, 4),)),
        "bias_position": centred(key_of[10], (D,), 0.5, 3.0, ((0, 4),)),
        "rel_proj": centred(key_of[11], (D, D), D ** -0.5, 0.1875, ((0, 4),)),
        "attn_proj": centred(key_of[12], (D, D), (D // 32) ** -0.5, 1.0, ((0, 4),)),
        "cross_gain": jnp.clip(1.0 + 0.18 * jax.random.normal(key_of[13], (D,), jnp.float32), 0.099609375, 1.8984375).astype(jnp.bfloat16),
        "cross_query": centred(key_of[14], (D, D), D ** -0.5, 0.1875, ((0, 4),)),
        "cross_key": centred(key_of[15], (D, D), D ** -0.5, 0.1875, ((0, 4),)),
        "cross_value": centred(key_of[16], (D, D), D ** -0.5, 0.1875, ((0, 4),)),
        "cross_proj": centred(key_of[17], (D, D), (D // 32) ** -0.5, 1.0, ((0, 4),)),
        "ffn_gain": jnp.clip(1.0 + 0.18 * jax.random.normal(key_of[18], (D,), jnp.float32), 0.099609375, 1.8984375).astype(jnp.bfloat16),
        "ffn_up": centred(key_of[19], (D, FF), D ** -0.5, 0.1875, ((0, 4),)),
        "ffn_down": centred(key_of[20], (FF, D), FF ** -0.5, 0.09375, ((0, 4),)),
    }


EPS = 1e-06
NEG = -1000000000.0
HIGH = lax.Precision.HIGHEST

@jax.custom_vjp
def low(v):
    return lax.optimization_barrier(v.astype(jnp.bfloat16)).astype(jnp.float32)

@jax.custom_vjp
def low_back(v):
    return v

def low_keep(v):
    return (low(v), None)

def low_pass(kept, grad):
    return (grad,)

def back_keep(v):
    return (v, None)

def back_low(kept, grad):
    return (low(grad),)
low.defvjp(low_keep, low_pass)
low_back.defvjp(back_keep, back_low)

def rounded_both(v):
    return low(low_back(v))

def matmul(left, right):
    return jnp.matmul(left, right, precision=HIGH)

def rms_norm(v, gain):
    factor = lax.rsqrt(lax.optimization_barrier(jnp.mean(v * v, axis=-1, keepdims=True)) + EPS)
    return v * factor * gain

def position_table(length, width):
    column = jnp.arange(length + BLOCK, dtype=jnp.float32)
    distance = length - 1 - column
    rates = jnp.exp(jnp.arange(width // 2, dtype=jnp.float32) * (-2.0 * math.log(10000.0) / width))
    angles = distance[:, None] * rates[None, :]
    return jnp.concatenate([jnp.sin(angles), jnp.cos(angles)], axis=1)

def rel_shift(full):
    lead = full.shape[:-2]
    length = full.shape[-2]
    span = full.shape[-1]
    flat = full.reshape(lead + (length * span,))
    piece = lax.slice_in_dim(flat, length - 1, length - 1 + length * (span - 1), axis=flat.ndim - 1)
    return piece.reshape(lead + (length, span - 1))[..., :length]

def block_mask(docs):
    length = docs.shape[-1]
    place = jnp.arange(length, dtype=jnp.int32) // BLOCK
    same = docs[:, :, None] == docs[:, None, :]
    earlier = place[None, :] <= place[:, None]
    return (same & earlier[None])[:, None]

def shift_rows(v):
    filler = jnp.zeros((v.shape[0], STRETCH - 1, v.shape[2]), v.dtype)
    return jnp.concatenate([v[:, STRETCH - 1:], filler], axis=1)

def unshift_rows(v):
    filler = jnp.zeros((v.shape[0], STRETCH - 1, v.shape[2]), v.dtype)
    return jnp.concatenate([filler, v[:, :v.shape[1] - STRETCH + 1]], axis=1)

def forward(tokens, near, docs, params):
    attn_gain, attn_query, attn_key, attn_value, bias_content, bias_position, rel_proj, attn_proj, cross_gain, cross_query, cross_key, cross_value, cross_proj, ffn_gain, ffn_up, ffn_down = params
    groups, length, width = tokens.shape
    stretches = length // STRETCH
    shape = (groups, length, HEADS, HDIM)
    qshape = (groups, stretches, STRETCH, HEADS, HDIM)
    kshape = (groups, stretches, NEIGH * NLEN, HEADS, HDIM)
    scale = HDIM ** (-0.5)
    normed = low(rms_norm(tokens, attn_gain))
    query = low_back(matmul(normed, attn_query))
    key = rounded_both(matmul(normed, attn_key))
    value = rounded_both(matmul(normed, attn_value))
    table = low(position_table(length, width))
    rel_key = rounded_both(matmul(jnp.broadcast_to(table, (groups,) + table.shape), rel_proj))
    content_q = low(query + bias_content)
    position_q = low(query + bias_position)
    content = jnp.einsum('gqhd,gkhd->ghqk', content_q.reshape(shape), key.reshape(shape), precision=HIGH)
    full = jnp.einsum('gqhd,grhd->ghqr', position_q.reshape(shape), rel_key.reshape(groups, -1, HEADS, HDIM), precision=HIGH)
    scores = low_back((content + rel_shift(full)) * scale)
    scores = jnp.where(block_mask(docs), scores, NEG)
    probs = low(jax.nn.softmax(scores, axis=-1))
    mixed = rounded_both(jnp.einsum('ghqk,gkhd->gqhd', probs, value.reshape(shape), precision=HIGH).reshape(groups, length, width))
    hidden = tokens + low_back(matmul(mixed, attn_proj))
    cnorm = shift_rows(low(rms_norm(hidden, cross_gain)))
    cquery = rounded_both(matmul(cnorm, cross_query)).reshape(qshape)
    ckey = rounded_both(matmul(near, cross_key)).reshape(kshape)
    cvalue = rounded_both(matmul(near, cross_value)).reshape(kshape)
    cscores = low_back(jnp.einsum('gcqhd,gckhd->gchqk', cquery, ckey, precision=HIGH) * scale)
    cprobs = low(jax.nn.softmax(cscores, axis=-1))
    cmixed = rounded_both(jnp.einsum('gchqk,gckhd->gcqhd', cprobs, cvalue, precision=HIGH).reshape(groups, length, width))
    hidden2 = hidden + low_back(unshift_rows(matmul(cmixed, cross_proj)))
    fnorm = low(rms_norm(hidden2, ffn_gain))
    upper = low_back(matmul(fnorm, ffn_up))
    active = low(jax.nn.gelu(upper))
    return hidden2 + low_back(matmul(active, ffn_down))

def reference(tokens, doc_ids, neighbours, neighbour_rows, out_grad, attn_gain, attn_query, attn_key, attn_value, bias_content, bias_position, rel_proj, attn_proj, cross_gain, cross_query, cross_key, cross_value, cross_proj, ffn_gain, ffn_up, ffn_down):
    params = tuple((weight.astype(jnp.float32) for weight in (attn_gain, attn_query, attn_key, attn_value, bias_content, bias_position, rel_proj, attn_proj, cross_gain, cross_query, cross_key, cross_value, cross_proj, ffn_gain, ffn_up, ffn_down)))
    seqs, length, width = tokens.shape
    stretches = length // STRETCH
    group = math.gcd(seqs, 4)
    turns = seqs // group
    items = (tokens.reshape(turns, group, length, width), doc_ids.reshape(turns, group, length), neighbour_rows.reshape(turns, group * stretches * NEIGH), out_grad.reshape(turns, group, length, width))

    def step(carry, item):
        part_tokens, part_docs, part_rows, part_grad = item
        near = neighbours[part_rows].astype(jnp.float32).reshape(group, stretches, NEIGH * NLEN, width)

        def run(inputs, nearby, weights):
            return forward(inputs, nearby, part_docs, weights)
        result, pull = jax.vjp(run, part_tokens.astype(jnp.float32), near, params)
        grad_x, grad_near, grad_params = pull(part_grad.astype(jnp.float32))
        carry = tuple((total + piece for total, piece in zip(carry, grad_params)))
        return (carry, (result.astype(jnp.bfloat16), grad_x.astype(jnp.bfloat16), grad_near.astype(jnp.bfloat16).reshape(-1, NLEN, width)))
    zeros = tuple((jnp.zeros(weight.shape, jnp.float32) for weight in params))
    totals, (results, grad_xs, grad_nears) = lax.scan(step, zeros, items)
    near_grad = jnp.zeros(neighbours.shape, jnp.bfloat16).at[neighbour_rows.reshape(-1).astype(jnp.int32)].add(grad_nears.reshape(-1, NLEN, width))
    return (results.reshape(tokens.shape), grad_xs.reshape(tokens.shape), near_grad, totals[0], totals[1], totals[2], totals[3], totals[4], totals[5], totals[6], totals[7], totals[8], totals[9], totals[10], totals[11], totals[12], totals[13], totals[14], totals[15])
```

```python
import math
from functools import partial
import jax
import jax.numpy as jnp
from jax import lax
from jax.sharding import PartitionSpec as P
from jax.experimental import pallas as pl
from jax.experimental.pallas import tpu as pltpu

HEADS = 14
HDIM = 64
STRETCH = 64
NEIGH = 2
NLEN = 128
BLOCK = 256
LANES = 128
EPS = 1e-06
NEG = -1000000000.0
SCALE = HDIM ** -0.5
F32 = jnp.float32
BF16 = jnp.bfloat16


def mm(a, b, ca, cb):
    return lax.dot_general(a, b, (((ca,), (cb,)), ((), ())), preferred_element_type=F32)


def low_lanes(shape):
    return lax.broadcasted_iota(jnp.int32, shape, len(shape) - 1) < HDIM


def self_fwd_kernel(q_ref, bc_ref, bp_ref, k_ref, v_ref, rel_ref, dr_ref, dc_ref, mixed_ref, *p_refs):
    length = k_ref.shape[0]
    query = q_ref[...]
    content_q = (query + bc_ref[...]).astype(BF16)
    position_q = (query + bp_ref[...]).astype(BF16)
    lo = low_lanes((1, LANES))
    masks = (lo, jnp.logical_not(lo))
    for index in range(length // BLOCK):
        first = index * BLOCK
        keys = first + BLOCK
        span = keys + BLOCK
        rel = rel_ref[length - keys : length - keys + span, :]
        cq = content_q[first:keys] * BF16(SCALE)
        pq = position_q[first:keys] * BF16(SCALE)
        same = dc_ref[0, first:keys, :] == dr_ref[0, :, :keys]
        outs = []
        for head in range(2):
            zero = jnp.zeros((), BF16)
            content = mm(jnp.where(masks[head], cq, zero), k_ref[:keys, :], 1, 1)
            full = mm(jnp.where(masks[head], pq, zero), rel, 1, 1)
            moved = pltpu.roll(full, span - BLOCK + 1, 1, stride=1, stride_axis=0)
            s = jnp.where(same, content + moved[:, :keys], NEG)
            e = jnp.exp(s - jnp.max(s, axis=1, keepdims=True))
            p = (e * (1.0 / jnp.sum(e, axis=1, keepdims=True))).astype(BF16)
            p_refs[index][0, 0, head] = p
            outs.append(mm(p, v_ref[:keys, :], 1, 0))
        mixed_ref[first:keys, :] = jnp.where(lo, outs[0], outs[1]).astype(BF16)


def self_bwd_kernel(q_ref, bc_ref, bp_ref, k_ref, v_ref, rel_ref, gm_ref, *refs):
    nblk = k_ref.shape[0] // BLOCK
    p_refs = refs[:nblk]
    gq_ref, gk_ref, gv_ref, grel_ref, gbc_ref, gbp_ref = refs[nblk : nblk + 6]
    gvt, gkt, grelt = refs[nblk + 6 :]
    length = k_ref.shape[0]
    seq = pl.program_id(1)
    query = q_ref[...]
    content_q = (query + bc_ref[...]).astype(BF16)
    position_q = (query + bp_ref[...]).astype(BF16)
    flip = (
        lax.broadcasted_iota(jnp.int32, (BLOCK, BLOCK), 0) + lax.broadcasted_iota(jnp.int32, (BLOCK, BLOCK), 1)
        == BLOCK - 1
    ).astype(BF16)
    gm = gm_ref[...]
    gmt = jnp.transpose(gm.astype(F32)).astype(BF16)
    lo = low_lanes((1, LANES))
    masks = (lo, jnp.logical_not(lo))
    zero = jnp.zeros((), BF16)
    gvt[...] = jnp.zeros_like(gvt)
    gkt[...] = jnp.zeros_like(gkt)
    grelt[...] = jnp.zeros_like(grelt)
    sum_c = jnp.zeros((1, LANES), F32)
    sum_p = jnp.zeros((1, LANES), F32)
    for index in range(nblk):
        first = index * BLOCK
        keys = first + BLOCK
        span = keys + BLOCK
        start = length - keys
        rel = rel_ref[start : start + span, :]
        gm_r = mm(flip, gm[first:keys], 1, 0).astype(BF16)
        cqt = jnp.transpose(mm(flip, content_q[first:keys] * BF16(SCALE), 1, 0)).astype(BF16)
        pqt = jnp.transpose(mm(flip, position_q[first:keys] * BF16(SCALE), 1, 0)).astype(BF16)
        gcs = []
        gps = []
        for head in range(2):
            hs = slice(head * HDIM, (head + 1) * HDIM)
            p = p_refs[index][0, 0, head]
            pf = mm(flip, p, 1, 0)
            g_p = mm(jnp.where(masks[head], gm_r, zero), v_ref[:keys, :], 1, 1)
            delta = jnp.sum(pf * g_p, axis=1, keepdims=True)
            gsf = pf * (g_p - delta)
            gs = gsf.astype(BF16)
            gvt[hs, :keys] += mm(gmt[hs, first:keys], p, 1, 0)
            gkt[hs, :keys] += mm(cqt[hs], gs, 1, 0)
            gcs.append(mm(gs, k_ref[:keys, :], 1, 0))
            padded = jnp.concatenate([gsf, jnp.zeros((BLOCK, BLOCK), F32)], axis=1)
            grel = pltpu.roll(padded, 0, 1, stride=1, stride_axis=0).astype(BF16)
            gps.append(mm(grel, rel, 1, 0))
            grelt[hs, start : start + span] += mm(pqt[hs], grel, 1, 0)
        gc = jnp.where(lo, gcs[0], gcs[1]) * SCALE
        gp = jnp.where(lo, gps[0], gps[1]) * SCALE
        sum_c += jnp.sum(gc, axis=0, keepdims=True)
        sum_p += jnp.sum(gp, axis=0, keepdims=True)
        gq_ref[first:keys, :] = mm(flip, (gc + gp).astype(BF16), 1, 0).astype(BF16)
    gv_ref[...] = jnp.transpose(gvt[...]).astype(BF16)
    gk_ref[...] = jnp.transpose(gkt[...]).astype(BF16)
    grel_ref[0] = jnp.transpose(grelt[...]).astype(BF16)

    @pl.when(seq == 0)
    def _():
        gbc_ref[...] = sum_c
        gbp_ref[...] = sum_p

    @pl.when(seq > 0)
    def _():
        gbc_ref[...] += sum_c
        gbp_ref[...] += sum_p


def self_specs(seqs, length, width):
    pairs = width // LANES
    table = length + BLOCK
    tok = pl.BlockSpec((length, LANES), lambda h, s: (s, h))
    vec = pl.BlockSpec((1, LANES), lambda h, s: (0, h))
    rel = pl.BlockSpec((table, LANES), lambda h, s: (0, h))
    probs = [
        pl.BlockSpec((1, 1, 2, BLOCK, (i + 1) * BLOCK), lambda h, s: (h, s, 0, 0, 0))
        for i in range(length // BLOCK)
    ]
    shapes = [
        jax.ShapeDtypeStruct((pairs, seqs, 2, BLOCK, (i + 1) * BLOCK), BF16)
        for i in range(length // BLOCK)
    ]
    return (pairs, seqs), tok, vec, rel, probs, shapes


def self_forward(query, bc, bp, key, value, rel_key, docs):
    seqs, length = docs.shape
    width = query.shape[1]
    grid, tok, vec, rel, pspecs, pshapes = self_specs(seqs, length, width)
    outs = pl.pallas_call(
        self_fwd_kernel,
        grid=grid,
        in_specs=[
            tok, vec, vec, tok, tok, rel,
            pl.BlockSpec((1, 1, length), lambda h, s: (s, 0, 0)),
            pl.BlockSpec((1, length, 1), lambda h, s: (s, 0, 0)),
        ],
        out_specs=[tok] + pspecs,
        out_shape=[jax.ShapeDtypeStruct(query.shape, BF16)] + pshapes,
        name="self_fwd",
    )(query, bc, bp, key, value, rel_key, docs[:, None, :], docs[:, :, None])
    return outs[0], outs[1:]


def self_backward(query, bc, bp, key, value, rel_key, g_mixed, probs):
    width = query.shape[1]
    seqs = probs[0].shape[1]
    length = query.shape[0] // seqs
    grid, tok, vec, rel, pspecs, _ = self_specs(seqs, length, width)
    table = length + BLOCK
    tshape = jax.ShapeDtypeStruct(query.shape, BF16)
    vshape = jax.ShapeDtypeStruct((1, width), F32)
    return pl.pallas_call(
        self_bwd_kernel,
        grid=grid,
        in_specs=[tok, vec, vec, tok, tok, rel, tok] + pspecs,
        out_specs=[tok, tok, tok, pl.BlockSpec((1, table, LANES), lambda h, s: (s, 0, h)), vec, vec],
        out_shape=[tshape, tshape, tshape, jax.ShapeDtypeStruct((seqs, table, width), BF16), vshape, vshape],
        scratch_shapes=[
            pltpu.VMEM((LANES, length), F32),
            pltpu.VMEM((LANES, length), F32),
            pltpu.VMEM((LANES, table), F32),
        ],
        name="self_bwd",
    )(query, bc, bp, key, value, rel_key, g_mixed, *probs)


def shift_up(v):
    return pltpu.roll(v, v.shape[0] - STRETCH + 1, 0)


def shift_down(v):
    moved = pltpu.roll(v, STRETCH - 1, 0)
    row = lax.broadcasted_iota(jnp.int32, (v.shape[0], 1), 0)
    return jnp.where(row >= STRETCH - 1, moved, 0.0)


def both_heads(v, lo):
    zero = jnp.zeros((), BF16)
    return jnp.concatenate([jnp.where(lo, v, zero), jnp.where(lo, zero, v)], axis=0)


def cross_fwd_kernel(rows_ref, q_ref, k0_ref, k1_ref, v0_ref, v1_ref, out_ref, p_ref, qs, os):
    u = pl.program_id(1)
    lo = low_lanes((1, LANES))

    @pl.when(u == 0)
    def _():
        qs[...] = shift_up(q_ref[...].astype(F32) * SCALE).astype(BF16)

    place = pl.ds(pl.multiple_of(u * STRETCH, STRETCH), STRETCH)
    for pair in range(q_ref.shape[1] // LANES):
        cols = slice(pair * LANES, (pair + 1) * LANES)
        q = both_heads(qs[place, cols], lo)
        k = jnp.concatenate([k0_ref[0, :, cols], k1_ref[0, :, cols]], axis=0)
        v = jnp.concatenate([v0_ref[0, :, cols], v1_ref[0, :, cols]], axis=0)
        s = mm(q, k, 1, 1)
        e = jnp.exp(s - jnp.max(s, axis=1, keepdims=True))
        p = (e * (1.0 / jnp.sum(e, axis=1, keepdims=True))).astype(BF16)
        p_ref[0, pair] = p
        o = mm(p, v, 1, 0)
        os[place, cols] = jnp.where(lo, o[:STRETCH], o[STRETCH:])

    @pl.when(u == pl.num_programs(1) - 1)
    def _():
        out_ref[...] = shift_down(os[...]).astype(BF16)


def cross_bwd_kernel(rows_ref, q_ref, g_ref, k0_ref, k1_ref, v0_ref, v1_ref, p_ref,
                     gq_ref, gk_ref, gv_ref, qs, gs_s, gq_s, gk_s, gv_s):
    u = pl.program_id(1)
    n = pl.program_id(2)
    lo = low_lanes((1, LANES))

    @pl.when(jnp.logical_and(u == 0, n == 0))
    def _():
        qs[...] = shift_up(q_ref[...].astype(F32) * SCALE).astype(BF16)
        g = g_ref[...].astype(F32)
        row = lax.broadcasted_iota(jnp.int32, (g.shape[0], 1), 0)
        gs_s[...] = shift_up(jnp.where(row >= STRETCH - 1, g, 0.0)).astype(BF16)

    @pl.when(n == 0)
    def _():
        place = pl.ds(pl.multiple_of(u * STRETCH, STRETCH), STRETCH)
        for pair in range(q_ref.shape[1] // LANES):
            cols = slice(pair * LANES, (pair + 1) * LANES)
            q = both_heads(qs[place, cols], lo)
            g = both_heads(gs_s[place, cols], lo)
            k = jnp.concatenate([k0_ref[0, :, cols], k1_ref[0, :, cols]], axis=0)
            v = jnp.concatenate([v0_ref[0, :, cols], v1_ref[0, :, cols]], axis=0)
            p = p_ref[0, pair]
            pf = p.astype(F32)
            g_p = mm(g, v, 1, 1)
            delta = jnp.sum(pf * g_p, axis=1, keepdims=True)
            gs = (pf * (g_p - delta)).astype(BF16)
            gv = mm(p, g, 0, 0).astype(BF16)
            gk = mm(gs, q, 0, 0).astype(BF16)
            gq = mm(gs, k, 1, 0)
            gq_s[place, cols] = jnp.where(lo, gq[:STRETCH], gq[STRETCH:]) * SCALE
            gk_ref[0, :, cols] = gk[:NLEN]
            gv_ref[0, :, cols] = gv[:NLEN]
            gk_s[:, cols] = gk[NLEN:]
            gv_s[:, cols] = gv[NLEN:]

    @pl.when(n == 1)
    def _():
        gk_ref[0] = gk_s[...]
        gv_ref[0] = gv_s[...]

    @pl.when(jnp.logical_and(u == pl.num_programs(1) - 1, n == 1))
    def _():
        gq_ref[...] = shift_down(gq_s[...]).astype(BF16)


def cross_forward(rows, cq, ck, cv, length):
    tokens, width = cq.shape
    seqs = tokens // length
    per = length // STRETCH
    pairs = width // LANES
    tok = pl.BlockSpec((length, width), lambda s, u, r: (s, 0))
    near = [
        pl.BlockSpec((1, NLEN, width), lambda s, u, r, n=n: (r[(s * per + u) * NEIGH + n], 0, 0))
        for n in range(NEIGH)
    ]
    return pl.pallas_call(
        cross_fwd_kernel,
        grid_spec=pltpu.PrefetchScalarGridSpec(
            num_scalar_prefetch=1,
            grid=(seqs, per),
            in_specs=[tok] + near + near,
            out_specs=[
                tok,
                pl.BlockSpec((1, pairs, 2 * STRETCH, NEIGH * NLEN), lambda s, u, r: (s * per + u, 0, 0, 0)),
            ],
            scratch_shapes=[pltpu.VMEM((length, width), BF16), pltpu.VMEM((length, width), F32)],
        ),
        out_shape=[
            jax.ShapeDtypeStruct(cq.shape, BF16),
            jax.ShapeDtypeStruct((seqs * per, pairs, 2 * STRETCH, NEIGH * NLEN), BF16),
        ],
        name="cross_fwd",
    )(rows, cq, ck, ck, cv, cv)


def cross_backward(rows, cq, g_cmixed, ck, cv, probs, length):
    tokens, width = cq.shape
    seqs = tokens // length
    per = length // STRETCH
    pairs = width // LANES
    tok = pl.BlockSpec((length, width), lambda s, u, n, r: (s, 0))
    near = [
        pl.BlockSpec((1, NLEN, width), lambda s, u, n, r, m=m: (r[(s * per + u) * NEIGH + m], 0, 0))
        for m in range(NEIGH)
    ]
    out = pl.BlockSpec((1, NLEN, width), lambda s, u, n, r: (r[(s * per + u) * NEIGH + n], 0, 0))
    return pl.pallas_call(
        cross_bwd_kernel,
        grid_spec=pltpu.PrefetchScalarGridSpec(
            num_scalar_prefetch=1,
            grid=(seqs, per, NEIGH),
            in_specs=[tok, tok] + near + near + [
                pl.BlockSpec((1, pairs, 2 * STRETCH, NEIGH * NLEN), lambda s, u, n, r: (s * per + u, 0, 0, 0)),
            ],
            out_specs=[tok, out, out],
            scratch_shapes=[
                pltpu.VMEM((length, width), BF16),
                pltpu.VMEM((length, width), BF16),
                pltpu.VMEM((length, width), F32),
                pltpu.VMEM((NLEN, width), BF16),
                pltpu.VMEM((NLEN, width), BF16),
            ],
        ),
        out_shape=[
            jax.ShapeDtypeStruct(cq.shape, BF16),
            jax.ShapeDtypeStruct(ck.shape, BF16),
            jax.ShapeDtypeStruct(cv.shape, BF16),
        ],
        name="cross_bwd",
    )(rows, cq, g_cmixed, ck, ck, cv, cv, probs)


def lowered(v):
    return v.astype(BF16)

def norm_factor(v):
    return lax.rsqrt(jnp.mean(v * v, axis=-1, keepdims=True) + EPS)

def norm_back(v, gain, gy):
    r = norm_factor(v)
    part = gain * gy
    gain_part = jnp.sum(gy * v * r, axis=0)
    return r * part - v * (r * r * r) * jnp.mean(part * v, axis=-1, keepdims=True), gain_part

def position_table(length, width):
    column = jnp.arange(length + BLOCK, dtype=F32)
    distance = length - 1 - column
    rates = jnp.exp(jnp.arange(width // 2, dtype=F32) * (-2.0 * math.log(10000.0) / width))
    angles = distance[:, None] * rates[None, :]
    return jnp.concatenate([jnp.sin(angles), jnp.cos(angles)], axis=1)

def layer(weights, tokens, docs, neighbours, rows, out_grad):
    (attn_gain, attn_query, attn_key, attn_value, bias_content, bias_position, rel_proj, attn_proj,
     cross_gain, cross_query, cross_key, cross_value, cross_proj, ffn_gain, ffn_up, ffn_down) = weights
    seqs, length, width = tokens.shape
    count = seqs * length
    near = neighbours.reshape(-1, width)
    kshape = neighbours.shape
    ag = attn_gain.astype(F32)
    cg = cross_gain.astype(F32)
    fg = ffn_gain.astype(F32)
    bc = bias_content.astype(F32)[None]
    bp = bias_position.astype(F32)[None]
    table = lowered(position_table(length, width))
    x = tokens.reshape(count, width).astype(F32)
    normed = lowered(x * norm_factor(x) * ag)
    query = mm(normed, attn_query, 1, 0)
    key = lowered(mm(normed, attn_key, 1, 0))
    value = lowered(mm(normed, attn_value, 1, 0))
    rel_key = lowered(mm(table, rel_proj, 1, 0))
    mixed, probs = self_forward(query, bc, bp, key, value, rel_key, docs)
    ck = lowered(mm(near, cross_key, 1, 0)).reshape(kshape)
    cv = lowered(mm(near, cross_value, 1, 0)).reshape(kshape)
    hidden = x + mm(mixed, attn_proj, 1, 0)
    cnorm = lowered(hidden * norm_factor(hidden) * cg)
    cq = lowered(mm(cnorm, cross_query, 1, 0))
    cmixed, cprobs = cross_forward(rows, cq, ck, cv, length)
    hidden2 = hidden + mm(cmixed, cross_proj, 1, 0)
    fnorm = lowered(hidden2 * norm_factor(hidden2) * fg)
    upper = mm(fnorm, ffn_up, 1, 0)
    active = lowered(jax.nn.gelu(upper))
    result = lowered(hidden2 + mm(active, ffn_down, 1, 0))
    gy = out_grad.reshape(count, width)
    g_down = mm(active, gy, 0, 0)
    g_active = mm(gy, ffn_down, 1, 1)
    g_upper = lowered(jax.vjp(jax.nn.gelu, upper)[1](g_active)[0])
    g_up = mm(fnorm, g_upper, 0, 0)
    g_fnorm = mm(g_upper, ffn_up, 1, 1)
    part, g_fg = norm_back(hidden2, fg, g_fnorm)
    g_h2 = gy.astype(F32) + part
    g_branch = lowered(g_h2)
    g_cproj = mm(cmixed, g_branch, 0, 0)
    g_cmixed = lowered(mm(g_branch, cross_proj, 1, 1))
    g_cq, g_ck, g_cv = cross_backward(rows, cq, g_cmixed, ck, cv, cprobs, length)
    g_ck2 = g_ck.reshape(near.shape)
    g_cv2 = g_cv.reshape(near.shape)
    g_cquery_w = mm(cnorm, g_cq, 0, 0)
    g_ckey_w = mm(near, g_ck2, 0, 0)
    g_cvalue_w = mm(near, g_cv2, 0, 0)
    g_near = lowered(mm(g_ck2, cross_key, 1, 1) + mm(g_cv2, cross_value, 1, 1)).reshape(kshape)
    g_cnorm = mm(g_cq, cross_query, 1, 1)
    part, g_cg = norm_back(hidden, cg, g_cnorm)
    g_h1 = g_h2 + part
    g_attn = lowered(g_h1)
    g_aproj = mm(mixed, g_attn, 0, 0)
    g_mixed = lowered(mm(g_attn, attn_proj, 1, 1))
    g_q, g_k, g_v, g_relk, g_bc, g_bp = self_backward(query, bc, bp, key, value, rel_key, g_mixed, probs)
    g_rel_sum = lowered(jnp.sum(g_relk.astype(F32), axis=0))
    g_rel = mm(table, g_rel_sum, 0, 0)
    g_query_w = mm(normed, g_q, 0, 0)
    g_key_w = mm(normed, g_k, 0, 0)
    g_value_w = mm(normed, g_v, 0, 0)
    g_normed = mm(g_q, attn_query, 1, 1) + mm(g_k, attn_key, 1, 1) + mm(g_v, attn_value, 1, 1)
    part, g_ag = norm_back(x, ag, g_normed)
    grad_x = lowered(g_h1 + part)
    grads = (g_ag, g_query_w, g_key_w, g_value_w, g_bc[0], g_bp[0], g_rel, g_aproj, g_cg, g_cquery_w,
             g_ckey_w, g_cvalue_w, g_cproj, g_fg, g_up, g_down)
    return (result.reshape(tokens.shape), grad_x.reshape(tokens.shape), g_near) + grads


SIDE = 8
VECTORS = (0, 4, 5, 8, 13)
SINGLE = (12,)
SETS = ((1, 2, 3, 6), (10, 11, 7, 9), (14,), (15,))


def split_set(arrays):
    parts = []
    for a in arrays:
        rows, cols = a.shape
        if cols > rows:
            a = a.reshape(rows, cols // 896, 896).swapaxes(0, 1)
        parts.append(a.reshape(-1, a.shape[-1]))
    return jnp.concatenate(parts, axis=0) if len(parts) > 1 else parts[0]


def gather_weights(local, reps, groups):
    full = [None] * len(local)
    small = jnp.stack([local[i] for i in VECTORS])
    small = lax.all_gather(small, "grp", axis=0)
    small = small.swapaxes(0, 1).reshape(len(VECTORS), -1)
    for n, i in enumerate(VECTORS):
        full[i] = small[n]
    me = lax.axis_index("rep")
    for i in SINGLE:
        full[i] = lax.all_gather(local[i], "grp", axis=0, tiled=True)
    for members in SETS:
        if reps != SIDE:
            for i in members:
                full[i] = lax.all_gather(local[i], "grp", axis=0, tiled=True)
            continue
        flat = split_set([local[i] for i in members])
        width = flat.shape[1]
        pieces = flat.reshape(SIDE, -1, width)
        mine = lax.dynamic_index_in_dim(pieces, me, 0, keepdims=False)
        got = lax.all_gather(mine, ("rep", "grp"), axis=0, tiled=True)
        high = mine.shape[0]
        if len(members) > 1:
            each = SIDE // len(members)
            got = got.reshape(len(members), each, groups, high, width)
            got = got.swapaxes(1, 2).reshape(len(members), -1, width)
            for n, i in enumerate(members):
                full[i] = got[n]
        else:
            i = members[0]
            rows, cols = local[i].shape
            blocks = cols // width
            got = got.reshape(blocks, SIDE // blocks, groups, high, width)
            full[i] = got.transpose(2, 1, 3, 0, 4).reshape(groups * rows, cols)
    return full


def reduce_grads(grads, reps, groups):
    out = [None] * len(grads)
    small = lax.psum(jnp.stack([grads[i] for i in VECTORS]), ("rep", "grp"))
    piece = small.shape[1] // groups
    small = lax.dynamic_slice_in_dim(small, lax.axis_index("grp") * piece, piece, axis=1)
    for n, i in enumerate(VECTORS):
        out[i] = small[n]
    for i in SINGLE:
        part = lax.psum_scatter(lowered(grads[i]), "grp", scatter_dimension=0, tiled=True)
        out[i] = lax.psum(part.astype(F32), "rep")
    for members in reversed(SETS):
        if reps != SIDE:
            for i in members:
                part = lax.psum_scatter(lowered(grads[i]), "grp", scatter_dimension=0, tiled=True)
                out[i] = lax.psum(part.astype(F32), "rep")
            continue
        parts = []
        for i in members:
            g = lowered(grads[i])
            rows, cols = g.shape
            width = min(rows, cols)
            high = rows * cols // (SIDE * groups * width) * (len(members))
            blocks = cols // width
            g = g.reshape(groups, -1, high, blocks, width).transpose(3, 1, 0, 2, 4)
            parts.append(g.reshape(-1, groups, high, width))
        whole = jnp.concatenate(parts, axis=0) if len(parts) > 1 else parts[0]
        whole = whole.reshape(-1, whole.shape[-1])
        part = lax.psum_scatter(whole, "rep", scatter_dimension=0, tiled=True)
        part = lax.psum_scatter(part, "grp", scatter_dimension=0, tiled=True)
        got = lax.all_gather(part, "rep", axis=0)
        for n, i in enumerate(members):
            rows, cols = grads[i].shape
            rows //= groups
            if len(members) > 1:
                each = SIDE // len(members)
                out[i] = got[n * each : (n + 1) * each].reshape(rows, cols).astype(F32)
            else:
                width = got.shape[-1]
                blocks = cols // width
                out[i] = got.reshape(blocks, rows, width).swapaxes(0, 1).reshape(rows, cols).astype(F32)
    return out


def per_device(mesh_shape, tokens, doc_ids, neighbours, neighbour_rows, out_grad, *local):
    reps, groups = mesh_shape
    rows = neighbour_rows.reshape(-1) % neighbours.shape[0]
    weights = gather_weights(local, reps, groups)
    outs = layer(weights, tokens, doc_ids, neighbours, rows, out_grad)
    return tuple(outs[:3]) + tuple(reduce_grads(outs[3:], reps, groups))


def solution(mesh):
    data3 = P(("rep", "grp"), None, None)
    data2 = P(("rep", "grp"), None)
    ranks = (1, 2, 2, 2, 1, 1, 2, 2, 1, 2, 2, 2, 2, 1, 2, 2)
    weights = tuple(P("grp") if r == 1 else P("grp", None) for r in ranks)
    return jax.shard_map(
        partial(per_device, (mesh.shape["rep"], mesh.shape["grp"])),
        mesh=mesh,
        in_specs=(data3, data2, data3, data2, data3) + weights,
        out_specs=(data3, data3, data3) + weights,
        check_vma=False,
    )
```

```python
import math
from functools import partial
import jax
import jax.numpy as jnp
from jax import lax
from jax.sharding import PartitionSpec as P
from jax.experimental import pallas as pl
from jax.experimental.pallas import tpu as pltpu

HEADS = 14
HDIM = 64
STRETCH = 64
NEIGH = 2
NLEN = 128
BLOCK = 256
LANES = 128
EPS = 1e-06
NEG = -1000000000.0
SCALE = HDIM ** -0.5
F32 = jnp.float32
BF16 = jnp.bfloat16


def mm(a, b, ca, cb):
    return lax.dot_general(a, b, (((ca,), (cb,)), ((), ())), preferred_element_type=F32)


def low_lanes(shape):
    return lax.broadcasted_iota(jnp.int32, shape, len(shape) - 1) < HDIM


def self_fwd_kernel(q_ref, bc_ref, bp_ref, k_ref, v_ref, rel_ref, dr_ref, dc_ref, mixed_ref, *p_refs):
    length = k_ref.shape[0]
    query = q_ref[...]
    content_q = (query + bc_ref[...]).astype(BF16)
    position_q = (query + bp_ref[...]).astype(BF16)
    lo = low_lanes((1, LANES))
    masks = (lo, jnp.logical_not(lo))
    for index in range(length // BLOCK):
        first = index * BLOCK
        keys = first + BLOCK
        span = keys + BLOCK
        rel = rel_ref[length - keys : length - keys + span, :]
        cq = content_q[first:keys] * BF16(SCALE)
        pq = position_q[first:keys] * BF16(SCALE)
        same = dc_ref[0, first:keys, :] == dr_ref[0, :, :keys]
        outs = []
        for head in range(2):
            zero = jnp.zeros((), BF16)
            content = mm(jnp.where(masks[head], cq, zero), k_ref[:keys, :], 1, 1)
            full = mm(jnp.where(masks[head], pq, zero), rel, 1, 1)
            moved = pltpu.roll(full, span - BLOCK + 1, 1, stride=1, stride_axis=0)
            s = jnp.where(same, content + moved[:, :keys], NEG)
            e = jnp.exp(s - jnp.max(s, axis=1, keepdims=True))
            p = (e * (1.0 / jnp.sum(e, axis=1, keepdims=True))).astype(BF16)
            p_refs[index][0, 0, head] = p
            outs.append(mm(p, v_ref[:keys, :], 1, 0))
        mixed_ref[first:keys, :] = jnp.where(lo, outs[0], outs[1]).astype(BF16)


def self_bwd_kernel(q_ref, bc_ref, bp_ref, k_ref, v_ref, rel_ref, gm_ref, *refs):
    nblk = k_ref.shape[0] // BLOCK
    p_refs = refs[:nblk]
    gq_ref, gk_ref, gv_ref, grel_ref, gbc_ref, gbp_ref = refs[nblk : nblk + 6]
    gvt, gkt, grelt = refs[nblk + 6 :]
    length = k_ref.shape[0]
    seq = pl.program_id(1)
    query = q_ref[...]
    content_q = (query + bc_ref[...]).astype(BF16)
    position_q = (query + bp_ref[...]).astype(BF16)
    flip = (
        lax.broadcasted_iota(jnp.int32, (BLOCK, BLOCK), 0) + lax.broadcasted_iota(jnp.int32, (BLOCK, BLOCK), 1)
        == BLOCK - 1
    ).astype(BF16)
    gm = gm_ref[...]
    gmt = jnp.transpose(gm.astype(F32)).astype(BF16)
    lo = low_lanes((1, LANES))
    masks = (lo, jnp.logical_not(lo))
    zero = jnp.zeros((), BF16)
    gvt[...] = jnp.zeros_like(gvt)
    gkt[...] = jnp.zeros_like(gkt)
    grelt[...] = jnp.zeros_like(grelt)
    sum_c = jnp.zeros((1, LANES), F32)
    sum_p = jnp.zeros((1, LANES), F32)
    for index in range(nblk):
        first = index * BLOCK
        keys = first + BLOCK
        span = keys + BLOCK
        start = length - keys
        rel = rel_ref[start : start + span, :]
        gm_r = mm(flip, gm[first:keys], 1, 0).astype(BF16)
        cqt = jnp.transpose(mm(flip, content_q[first:keys] * BF16(SCALE), 1, 0)).astype(BF16)
        pqt = jnp.transpose(mm(flip, position_q[first:keys] * BF16(SCALE), 1, 0)).astype(BF16)
        gcs = []
        gps = []
        for head in range(2):
            hs = slice(head * HDIM, (head + 1) * HDIM)
            p = p_refs[index][0, 0, head]
            pf = mm(flip, p, 1, 0)
            g_p = mm(jnp.where(masks[head], gm_r, zero), v_ref[:keys, :], 1, 1)
            delta = jnp.sum(pf * g_p, axis=1, keepdims=True)
            gsf = pf * (g_p - delta)
            gs = gsf.astype(BF16)
            gvt[hs, :keys] += mm(gmt[hs, first:keys], p, 1, 0)
            gkt[hs, :keys] += mm(cqt[hs], gs, 1, 0)
            gcs.append(mm(gs, k_ref[:keys, :], 1, 0))
            padded = jnp.concatenate([gsf, jnp.zeros((BLOCK, BLOCK), F32)], axis=1)
            grel = pltpu.roll(padded, 0, 1, stride=1, stride_axis=0).astype(BF16)
            gps.append(mm(grel, rel, 1, 0))
            grelt[hs, start : start + span] += mm(pqt[hs], grel, 1, 0)
        gc = jnp.where(lo, gcs[0], gcs[1]) * SCALE
        gp = jnp.where(lo, gps[0], gps[1]) * SCALE
        sum_c += jnp.sum(gc, axis=0, keepdims=True)
        sum_p += jnp.sum(gp, axis=0, keepdims=True)
        gq_ref[first:keys, :] = mm(flip, (gc + gp).astype(BF16), 1, 0).astype(BF16)
    gv_ref[...] = jnp.transpose(gvt[...]).astype(BF16)
    gk_ref[...] = jnp.transpose(gkt[...]).astype(BF16)
    grel_ref[0] = jnp.transpose(grelt[...]).astype(BF16)

    @pl.when(seq == 0)
    def _():
        gbc_ref[...] = sum_c
        gbp_ref[...] = sum_p

    @pl.when(seq > 0)
    def _():
        gbc_ref[...] += sum_c
        gbp_ref[...] += sum_p


def self_specs(seqs, length, width):
    pairs = width // LANES
    table = length + BLOCK
    tok = pl.BlockSpec((length, LANES), lambda h, s: (s, h))
    vec = pl.BlockSpec((1, LANES), lambda h, s: (0, h))
    rel = pl.BlockSpec((table, LANES), lambda h, s: (0, h))
    probs = [
        pl.BlockSpec((1, 1, 2, BLOCK, (i + 1) * BLOCK), lambda h, s: (h, s, 0, 0, 0))
        for i in range(length // BLOCK)
    ]
    shapes = [
        jax.ShapeDtypeStruct((pairs, seqs, 2, BLOCK, (i + 1) * BLOCK), BF16)
        for i in range(length // BLOCK)
    ]
    return (pairs, seqs), tok, vec, rel, probs, shapes


def self_forward(query, bc, bp, key, value, rel_key, docs):
    seqs, length = docs.shape
    width = query.shape[1]
    grid, tok, vec, rel, pspecs, pshapes = self_specs(seqs, length, width)
    outs = pl.pallas_call(
        self_fwd_kernel,
        grid=grid,
        in_specs=[
            tok, vec, vec, tok, tok, rel,
            pl.BlockSpec((1, 1, length), lambda h, s: (s, 0, 0)),
            pl.BlockSpec((1, length, 1), lambda h, s: (s, 0, 0)),
        ],
        out_specs=[tok] + pspecs,
        out_shape=[jax.ShapeDtypeStruct(query.shape, BF16)] + pshapes,
        name="self_fwd",
    )(query, bc, bp, key, value, rel_key, docs[:, None, :], docs[:, :, None])
    return outs[0], outs[1:]


def self_backward(query, bc, bp, key, value, rel_key, g_mixed, probs):
    width = query.shape[1]
    seqs = probs[0].shape[1]
    length = query.shape[0] // seqs
    grid, tok, vec, rel, pspecs, _ = self_specs(seqs, length, width)
    table = length + BLOCK
    tshape = jax.ShapeDtypeStruct(query.shape, BF16)
    vshape = jax.ShapeDtypeStruct((1, width), F32)
    return pl.pallas_call(
        self_bwd_kernel,
        grid=grid,
        in_specs=[tok, vec, vec, tok, tok, rel, tok] + pspecs,
        out_specs=[tok, tok, tok, pl.BlockSpec((1, table, LANES), lambda h, s: (s, 0, h)), vec, vec],
        out_shape=[tshape, tshape, tshape, jax.ShapeDtypeStruct((seqs, table, width), BF16), vshape, vshape],
        scratch_shapes=[
            pltpu.VMEM((LANES, length), F32),
            pltpu.VMEM((LANES, length), F32),
            pltpu.VMEM((LANES, table), F32),
        ],
        name="self_bwd",
    )(query, bc, bp, key, value, rel_key, g_mixed, *probs)


def shift_up(v):
    return pltpu.roll(v, v.shape[0] - STRETCH + 1, 0)


def shift_down(v):
    moved = pltpu.roll(v, STRETCH - 1, 0)
    row = lax.broadcasted_iota(jnp.int32, (v.shape[0], 1), 0)
    return jnp.where(row >= STRETCH - 1, moved, 0.0)


def both_heads(v, lo):
    zero = jnp.zeros((), BF16)
    return jnp.concatenate([jnp.where(lo, v, zero), jnp.where(lo, zero, v)], axis=0)


def cross_fwd_kernel(rows_ref, q_ref, k0_ref, k1_ref, v0_ref, v1_ref, out_ref, p_ref, qs, os):
    u = pl.program_id(1)
    lo = low_lanes((1, LANES))

    @pl.when(u == 0)
    def _():
        qs[...] = shift_up(q_ref[...].astype(F32) * SCALE).astype(BF16)

    place = pl.ds(pl.multiple_of(u * STRETCH, STRETCH), STRETCH)
    for pair in range(q_ref.shape[1] // LANES):
        cols = slice(pair * LANES, (pair + 1) * LANES)
        q = both_heads(qs[place, cols], lo)
        k = jnp.concatenate([k0_ref[0, :, cols], k1_ref[0, :, cols]], axis=0)
        v = jnp.concatenate([v0_ref[0, :, cols], v1_ref[0, :, cols]], axis=0)
        s = mm(q, k, 1, 1)
        e = jnp.exp(s - jnp.max(s, axis=1, keepdims=True))
        p = (e * (1.0 / jnp.sum(e, axis=1, keepdims=True))).astype(BF16)
        p_ref[0, pair] = p
        o = mm(p, v, 1, 0)
        os[place, cols] = jnp.where(lo, o[:STRETCH], o[STRETCH:])

    @pl.when(u == pl.num_programs(1) - 1)
    def _():
        out_ref[...] = shift_down(os[...]).astype(BF16)


def cross_bwd_kernel(rows_ref, q_ref, g_ref, k0_ref, k1_ref, v0_ref, v1_ref, p_ref,
                     gq_ref, gk_ref, gv_ref, qs, gs_s, gq_s, gk_s, gv_s):
    u = pl.program_id(1)
    n = pl.program_id(2)
    lo = low_lanes((1, LANES))

    @pl.when(jnp.logical_and(u == 0, n == 0))
    def _():
        qs[...] = shift_up(q_ref[...].astype(F32) * SCALE).astype(BF16)
        g = g_ref[...].astype(F32)
        row = lax.broadcasted_iota(jnp.int32, (g.shape[0], 1), 0)
        gs_s[...] = shift_up(jnp.where(row >= STRETCH - 1, g, 0.0)).astype(BF16)

    @pl.when(n == 0)
    def _():
        place = pl.ds(pl.multiple_of(u * STRETCH, STRETCH), STRETCH)
        for pair in range(q_ref.shape[1] // LANES):
            cols = slice(pair * LANES, (pair + 1) * LANES)
            q = both_heads(qs[place, cols], lo)
            g = both_heads(gs_s[place, cols], lo)
            k = jnp.concatenate([k0_ref[0, :, cols], k1_ref[0, :, cols]], axis=0)
            v = jnp.concatenate([v0_ref[0, :, cols], v1_ref[0, :, cols]], axis=0)
            p = p_ref[0, pair]
            pf = p.astype(F32)
            g_p = mm(g, v, 1, 1)
            delta = jnp.sum(pf * g_p, axis=1, keepdims=True)
            gs = (pf * (g_p - delta)).astype(BF16)
            gv = mm(p, g, 0, 0).astype(BF16)
            gk = mm(gs, q, 0, 0).astype(BF16)
            gq = mm(gs, k, 1, 0)
            gq_s[place, cols] = jnp.where(lo, gq[:STRETCH], gq[STRETCH:]) * SCALE
            gk_ref[0, :, cols] = gk[:NLEN]
            gv_ref[0, :, cols] = gv[:NLEN]
            gk_s[:, cols] = gk[NLEN:]
            gv_s[:, cols] = gv[NLEN:]

    @pl.when(n == 1)
    def _():
        gk_ref[0] = gk_s[...]
        gv_ref[0] = gv_s[...]

    @pl.when(jnp.logical_and(u == pl.num_programs(1) - 1, n == 1))
    def _():
        gq_ref[...] = shift_down(gq_s[...]).astype(BF16)


def cross_forward(rows, cq, ck, cv, length):
    tokens, width = cq.shape
    seqs = tokens // length
    per = length // STRETCH
    pairs = width // LANES
    tok = pl.BlockSpec((length, width), lambda s, u, r: (s, 0))
    near = [
        pl.BlockSpec((1, NLEN, width), lambda s, u, r, n=n: (r[(s * per + u) * NEIGH + n], 0, 0))
        for n in range(NEIGH)
    ]
    return pl.pallas_call(
        cross_fwd_kernel,
        grid_spec=pltpu.PrefetchScalarGridSpec(
            num_scalar_prefetch=1,
            grid=(seqs, per),
            in_specs=[tok] + near + near,
            out_specs=[
                tok,
                pl.BlockSpec((1, pairs, 2 * STRETCH, NEIGH * NLEN), lambda s, u, r: (s * per + u, 0, 0, 0)),
            ],
            scratch_shapes=[pltpu.VMEM((length, width), BF16), pltpu.VMEM((length, width), F32)],
        ),
        out_shape=[
            jax.ShapeDtypeStruct(cq.shape, BF16),
            jax.ShapeDtypeStruct((seqs * per, pairs, 2 * STRETCH, NEIGH * NLEN), BF16),
        ],
        name="cross_fwd",
    )(rows, cq, ck, ck, cv, cv)


def cross_backward(rows, cq, g_cmixed, ck, cv, probs, length):
    tokens, width = cq.shape
    seqs = tokens // length
    per = length // STRETCH
    pairs = width // LANES
    tok = pl.BlockSpec((length, width), lambda s, u, n, r: (s, 0))
    near = [
        pl.BlockSpec((1, NLEN, width), lambda s, u, n, r, m=m: (r[(s * per + u) * NEIGH + m], 0, 0))
        for m in range(NEIGH)
    ]
    out = pl.BlockSpec((1, NLEN, width), lambda s, u, n, r: (r[(s * per + u) * NEIGH + n], 0, 0))
    return pl.pallas_call(
        cross_bwd_kernel,
        grid_spec=pltpu.PrefetchScalarGridSpec(
            num_scalar_prefetch=1,
            grid=(seqs, per, NEIGH),
            in_specs=[tok, tok] + near + near + [
                pl.BlockSpec((1, pairs, 2 * STRETCH, NEIGH * NLEN), lambda s, u, n, r: (s * per + u, 0, 0, 0)),
            ],
            out_specs=[tok, out, out],
            scratch_shapes=[
                pltpu.VMEM((length, width), BF16),
                pltpu.VMEM((length, width), BF16),
                pltpu.VMEM((length, width), F32),
                pltpu.VMEM((NLEN, width), BF16),
                pltpu.VMEM((NLEN, width), BF16),
            ],
        ),
        out_shape=[
            jax.ShapeDtypeStruct(cq.shape, BF16),
            jax.ShapeDtypeStruct(ck.shape, BF16),
            jax.ShapeDtypeStruct(cv.shape, BF16),
        ],
        name="cross_bwd",
    )(rows, cq, g_cmixed, ck, ck, cv, cv, probs)


def lowered(v):
    return v.astype(BF16)

def norm_factor(v):
    return lax.rsqrt(jnp.mean(v * v, axis=-1, keepdims=True) + EPS)

def norm_back(v, gain, gy):
    r = norm_factor(v)
    part = gain * gy
    gain_part = jnp.sum(gy * v * r, axis=0)
    return r * part - v * (r * r * r) * jnp.mean(part * v, axis=-1, keepdims=True), gain_part

def position_table(length, width):
    column = jnp.arange(length + BLOCK, dtype=F32)
    distance = length - 1 - column
    rates = jnp.exp(jnp.arange(width // 2, dtype=F32) * (-2.0 * math.log(10000.0) / width))
    angles = distance[:, None] * rates[None, :]
    return jnp.concatenate([jnp.sin(angles), jnp.cos(angles)], axis=1)

def layer(weights, tokens, docs, neighbours, rows, out_grad):
    (attn_gain, attn_query, attn_key, attn_value, bias_content, bias_position, rel_proj, attn_proj,
     cross_gain, cross_query, cross_key, cross_value, cross_proj, ffn_gain, ffn_up, ffn_down) = weights
    seqs, length, width = tokens.shape
    count = seqs * length
    near = neighbours.reshape(-1, width)
    kshape = neighbours.shape
    ag = attn_gain.astype(F32)
    cg = cross_gain.astype(F32)
    fg = ffn_gain.astype(F32)
    bc = bias_content.astype(F32)[None]
    bp = bias_position.astype(F32)[None]
    table = lowered(position_table(length, width))
    x = tokens.reshape(count, width).astype(F32)
    normed = lowered(x * norm_factor(x) * ag)
    query = mm(normed, attn_query, 1, 0)
    key = lowered(mm(normed, attn_key, 1, 0))
    value = lowered(mm(normed, attn_value, 1, 0))
    rel_key = lowered(mm(table, rel_proj, 1, 0))
    mixed, probs = self_forward(query, bc, bp, key, value, rel_key, docs)
    ck = lowered(mm(near, cross_key, 1, 0)).reshape(kshape)
    cv = lowered(mm(near, cross_value, 1, 0)).reshape(kshape)
    hidden = x + mm(mixed, attn_proj, 1, 0)
    cnorm = lowered(hidden * norm_factor(hidden) * cg)
    cq = lowered(mm(cnorm, cross_query, 1, 0))
    cmixed, cprobs = cross_forward(rows, cq, ck, cv, length)
    hidden2 = hidden + mm(cmixed, cross_proj, 1, 0)
    fnorm = lowered(hidden2 * norm_factor(hidden2) * fg)
    upper = mm(fnorm, ffn_up, 1, 0)
    active = lowered(jax.nn.gelu(upper))
    result = lowered(hidden2 + mm(active, ffn_down, 1, 0))
    gy = out_grad.reshape(count, width)
    g_down = mm(active, gy, 0, 0)
    g_active = mm(gy, ffn_down, 1, 1)
    g_upper = lowered(jax.vjp(jax.nn.gelu, upper)[1](g_active)[0])
    g_up = mm(fnorm, g_upper, 0, 0)
    g_fnorm = mm(g_upper, ffn_up, 1, 1)
    part, g_fg = norm_back(hidden2, fg, g_fnorm)
    g_h2 = gy.astype(F32) + part
    g_branch = lowered(g_h2)
    g_cproj = mm(cmixed, g_branch, 0, 0)
    g_cmixed = lowered(mm(g_branch, cross_proj, 1, 1))
    g_cq, g_ck, g_cv = cross_backward(rows, cq, g_cmixed, ck, cv, cprobs, length)
    g_ck2 = g_ck.reshape(near.shape)
    g_cv2 = g_cv.reshape(near.shape)
    g_cquery_w = mm(cnorm, g_cq, 0, 0)
    g_ckey_w = mm(near, g_ck2, 0, 0)
    g_cvalue_w = mm(near, g_cv2, 0, 0)
    g_near = lowered(mm(g_ck2, cross_key, 1, 1) + mm(g_cv2, cross_value, 1, 1)).reshape(kshape)
    g_cnorm = mm(g_cq, cross_query, 1, 1)
    part, g_cg = norm_back(hidden, cg, g_cnorm)
    g_h1 = g_h2 + part
    g_attn = lowered(g_h1)
    g_aproj = mm(mixed, g_attn, 0, 0)
    g_mixed = lowered(mm(g_attn, attn_proj, 1, 1))
    g_q, g_k, g_v, g_relk, g_bc, g_bp = self_backward(query, bc, bp, key, value, rel_key, g_mixed, probs)
    g_rel_sum = lowered(jnp.sum(g_relk.astype(F32), axis=0))
    g_rel = mm(table, g_rel_sum, 0, 0)
    g_query_w = mm(normed, g_q, 0, 0)
    g_key_w = mm(normed, g_k, 0, 0)
    g_value_w = mm(normed, g_v, 0, 0)
    g_normed = mm(g_q, attn_query, 1, 1) + mm(g_k, attn_key, 1, 1) + mm(g_v, attn_value, 1, 1)
    part, g_ag = norm_back(x, ag, g_normed)
    grad_x = lowered(g_h1 + part)
    grads = (g_ag, g_query_w, g_key_w, g_value_w, g_bc[0], g_bp[0], g_rel, g_aproj, g_cg, g_cquery_w,
             g_ckey_w, g_cvalue_w, g_cproj, g_fg, g_up, g_down)
    return (result.reshape(tokens.shape), grad_x.reshape(tokens.shape), g_near) + grads


SIDE = 8
CHIPS = 4
PARTS = 4
VECTORS = (0, 4, 5, 8, 13)
SINGLE = 12
SETS = ((1, 2, 3, 6), (10, 11, 7, 9), (14,), (15,))


def swap(v, bits):
    return lax.ppermute(v, "rep", [(r, r ^ bits) for r in range(SIDE)])


def shift(v, step):
    return lax.ppermute(v, "grp", [(g, (g + step) % PARTS) for g in range(PARTS)])


def total(parts):
    out = parts[0].astype(F32)
    for part in parts[1:]:
        out = out + part.astype(F32)
    return out


class Place:
    def __init__(self):
        me = lax.axis_index("rep")
        self.core = me % 2
        self.chip = me // 2
        self.grp = lax.axis_index("grp")
        self.table = jnp.stack(
            [jnp.bitwise_xor(self.chip, u) for u in range(CHIPS)]
            + [(self.grp + PARTS - s) % PARTS for s in range(PARTS)]
            + [self.core]
        ).astype(jnp.int32)


def assemble_kernel(kind, meta, *refs):
    local = {"four": 4}.get(kind, 1)
    locals_, (mine, other) = refs[:local], refs[local : local + 2]
    outs, sems = refs[local + 2 : -1], refs[-1]
    high = mine.shape[2]
    width = mine.shape[3]
    here = meta[CHIPS]
    core = meta[CHIPS + PARTS]
    copies = []

    def add(src, dst):
        copies.append(pltpu.make_async_copy(src, dst, sems.at[len(copies)]))

    for i in range(local):
        rows = locals_[i].shape[0]
        add(locals_[i], outs[i].at[pl.ds(pl.multiple_of(here * rows, 16), rows)])
    for u in range(CHIPS):
        for s in range(1, PARTS):
            k = meta[CHIPS + s]
            for flip, src in ((0, mine), (1, other)):
                half = core if flip == 0 else 1 - core
                if kind == "four":
                    dst = outs[u].at[pl.ds(pl.multiple_of(k * 2 * high + half * high, 16), high)]
                elif kind == "down":
                    row = k * CHIPS * 2 * high + u * 2 * high + half * high
                    dst = outs[0].at[pl.ds(pl.multiple_of(row, 16), high)]
                else:
                    row = pl.multiple_of(k * 2 * high + half * high, 16)
                    dst = outs[0].at[pl.ds(row, high), pl.ds(u * width, width)]
                add(src.at[meta[u], s - 1], dst)
    for copy in copies:
        copy.start()
    for copy in copies:
        copy.wait()


def assemble(kind, place, locals_, mine, other):
    hbm = pl.BlockSpec(memory_space=pl.ANY)
    shapes = [jax.ShapeDtypeStruct((PARTS * a.shape[0], a.shape[1]), a.dtype) for a in locals_]
    count = len(locals_) + 2 * CHIPS * (PARTS - 1)
    return pl.pallas_call(
        partial(assemble_kernel, kind),
        in_specs=[pl.BlockSpec(memory_space=pltpu.SMEM)] + [hbm] * (len(locals_) + 2),
        out_specs=[hbm] * len(shapes),
        out_shape=shapes,
        scratch_shapes=[pltpu.SemaphoreType.DMA((count,))],
        name="assemble_" + kind,
    )(place.table, *locals_, mine, other)


def pick(parts, index):
    out = parts[0]
    for n in range(1, len(parts)):
        out = jnp.where(index == n, parts[n], out)
    return out


def set_kind(members, local):
    if len(members) > 1:
        return "four"
    return "up" if local[members[0]].shape[1] > local[members[0]].shape[0] else "down"


def own_piece(kind, place, locals_):
    if kind == "four":
        high = locals_[0].shape[0] // 2
        return pick([lax.dynamic_slice_in_dim(a, place.core * high, high, 0) for a in locals_], place.chip)
    a = locals_[0]
    if kind == "down":
        high = a.shape[0] // SIDE
        return lax.dynamic_slice_in_dim(a, (place.chip * 2 + place.core) * high, high, 0)
    high, width = a.shape[0] // 2, a.shape[1] // CHIPS
    return lax.dynamic_slice(a, (place.core * high, place.chip * width), (high, width))


def gather_weights(local, reps, groups):
    full = [None] * len(local)
    if reps != SIDE or groups != PARTS:
        return [lax.all_gather(a, "grp", axis=0, tiled=True) for a in local]
    place = Place()
    small = jnp.stack([local[i] for i in VECTORS])
    slots = [small] + [shift(small, s) for s in range(1, PARTS)]
    slots = jnp.stack(slots)
    order = [lax.dynamic_index_in_dim(slots, (place.grp + PARTS - k) % PARTS, 0, keepdims=False) for k in range(PARTS)]
    small = jnp.concatenate(order, axis=1)
    for n, i in enumerate(VECTORS):
        full[i] = small[n]
    tie = small
    for number, members in enumerate(SETS):
        locals_ = [local[i] for i in members]
        kind = set_kind(members, local)
        own, tie = lax.optimization_barrier((own_piece(kind, place, locals_), tie))
        got = jnp.stack([shift(own, s) for s in range(1, PARTS)])
        tie = got
        mine = jnp.stack([got] + [swap(got, 2 * b) for b in range(1, CHIPS)])
        other = swap(mine, 1)
        outs = assemble(kind, place, locals_, mine, other)
        for i, w in zip(members, outs):
            full[i] = w
        if number == 1:
            a = local[SINGLE]
            high = a.shape[0] // 2
            own, tie = lax.optimization_barrier((lax.dynamic_slice_in_dim(a, place.core * high, high, 0), tie))
            got = [own] + [shift(own, s) for s in range(1, PARTS)]
            tie = got[1]
            mine = jnp.stack([lax.dynamic_index_in_dim(jnp.stack(got), (place.grp + PARTS - k) % PARTS, 0, keepdims=False) for k in range(PARTS)])
            other = swap(mine, 1)
            pair = jnp.stack([jnp.where(place.core == 0, mine, other), jnp.where(place.core == 0, other, mine)], axis=1)
            full[SINGLE] = pair.reshape(-1, a.shape[1])
    return full


def spread_kernel(meta, *refs):
    half = len(refs) // 2
    for n in range(half):
        refs[half + n][...] = refs[n][0, 0].astype(F32)


def spread(kind, place, stack, shapes):
    high, width = stack.shape[2:]
    block = (1, 1, high, width)
    if kind == "four":
        grid = (2,)
        ins = [pl.BlockSpec(block, lambda h, m, u=u: (m[u], jnp.bitwise_xor(h, m[CHIPS + PARTS]), 0, 0)) for u in range(CHIPS)]
        outs = [pl.BlockSpec((high, width), lambda h, m: (h, 0))] * CHIPS
    else:
        grid = (CHIPS, 2)
        ins = [pl.BlockSpec(block, lambda u, h, m: (m[u], jnp.bitwise_xor(h, m[CHIPS + PARTS]), 0, 0))]
        if kind == "down":
            outs = [pl.BlockSpec((high, width), lambda u, h, m: (2 * u + h, 0))]
        else:
            outs = [pl.BlockSpec((high, width), lambda u, h, m: (h, u))]
    return pl.pallas_call(
        spread_kernel,
        grid_spec=pltpu.PrefetchScalarGridSpec(num_scalar_prefetch=1, grid=grid, in_specs=ins, out_specs=outs),
        out_shape=[jax.ShapeDtypeStruct(s, F32) for s in shapes],
        name="spread_" + kind,
    )(place.table, *([stack] * len(ins)))


def grad_piece(kind, place, grads, unit, half):
    if kind == "four":
        a = grads[0]
        high = a.shape[3]
        out = lax.dynamic_slice(a, (unit, 0, half, 0, 0), (1, PARTS, 1, high, a.shape[4]))
        return out.reshape(PARTS, high, a.shape[4])
    rows, cols = grads[0].shape
    if kind == "down":
        high = rows // (PARTS * SIDE)
        a = grads[0].reshape(PARTS, SIDE, high, cols)
        return lax.dynamic_index_in_dim(a, 2 * unit + half, 1, keepdims=False)
    high, width = rows // (PARTS * 2), cols // CHIPS
    a = grads[0].reshape(PARTS, 2, high, cols)
    out = lax.dynamic_slice(a, (0, half, 0, unit * width), (PARTS, 1, high, width))
    return out.reshape(PARTS, high, width)


def scatter_grp(place, parts):
    send = [lax.dynamic_index_in_dim(parts, (place.grp + s) % PARTS, 0, keepdims=False) for s in range(PARTS)]
    return total([send[0]] + [shift(send[s], s) for s in range(1, PARTS)])


def reduce_set(kind, place, grads, shapes):
    if kind == "four":
        rows, cols = grads[0].shape
        grads = [jnp.stack(grads).reshape(CHIPS, PARTS, 2, rows // (2 * PARTS), cols)]
    units = [jnp.bitwise_xor(place.chip, b) for b in range(CHIPS)]
    send = jnp.stack([grad_piece(kind, place, grads, u, 1 - place.core) for u in units])
    got = swap(send, 1)
    sums = [lowered(total([grad_piece(kind, place, grads, u, place.core), got[b]])) for b, u in enumerate(units)]
    part = lowered(total([sums[0]] + [swap(sums[b], 2 * b) for b in range(1, CHIPS)]))
    mine = lowered(scatter_grp(place, part))
    mine = jnp.stack([mine] + [swap(mine, 2 * b) for b in range(1, CHIPS)])
    other = swap(mine, 1)
    return spread(kind, place, jnp.stack([mine, other], axis=1), shapes)


def reduce_single(place, grad):
    rows, cols = grad.shape
    a = grad.reshape(PARTS, 2, rows // (2 * PARTS), cols)
    got = swap(lax.dynamic_index_in_dim(a, 1 - place.core, 1, keepdims=False), 1)
    part = lowered(total([lax.dynamic_index_in_dim(a, place.core, 1, keepdims=False), got]))
    mine = lowered(scatter_grp(place, part))
    mine = lowered(total([mine] + [swap(mine, 2 * b) for b in range(1, CHIPS)]))
    other = swap(mine, 1)
    first = jnp.where(place.core == 0, mine, other)
    second = jnp.where(place.core == 0, other, mine)
    return jnp.concatenate([first, second], axis=0).astype(F32)


def reduce_vectors(place, small):
    for bits in (1, 2, 4):
        small = small + swap(small, bits)
    for bits in (1, 2):
        small = small + lax.ppermute(small, "grp", [(g, g ^ bits) for g in range(PARTS)])
    piece = small.shape[1] // PARTS
    return lax.dynamic_slice_in_dim(small, place.grp * piece, piece, axis=1)


def reduce_grads(grads, reps, groups):
    out = [None] * len(grads)
    if reps != SIDE or groups != PARTS:
        for i, g in enumerate(grads):
            part = lax.psum_scatter(lowered(g), "grp", scatter_dimension=0, tiled=True)
            out[i] = lax.psum(part.astype(F32), "rep")
        return out
    place = Place()
    small = reduce_vectors(place, jnp.stack([grads[i] for i in VECTORS]))
    for n, i in enumerate(VECTORS):
        out[i] = small[n]
    out[SINGLE] = reduce_single(place, lowered(grads[SINGLE]))
    for members in reversed(SETS):
        low = [lowered(grads[i]) for i in members]
        kind = set_kind(members, grads)
        shapes = [(a.shape[0] // PARTS, a.shape[1]) for a in low]
        for i, w in zip(members, reduce_set(kind, place, low, shapes)):
            out[i] = w
    return out


def per_device(mesh_shape, tokens, doc_ids, neighbours, neighbour_rows, out_grad, *local):
    reps, groups = mesh_shape
    rows = neighbour_rows.reshape(-1) % neighbours.shape[0]
    weights = gather_weights(local, reps, groups)
    outs = layer(weights, tokens, doc_ids, neighbours, rows, out_grad)
    return tuple(outs[:3]) + tuple(reduce_grads(outs[3:], reps, groups))


def solution(mesh):
    data3 = P(("rep", "grp"), None, None)
    data2 = P(("rep", "grp"), None)
    ranks = (1, 2, 2, 2, 1, 1, 2, 2, 1, 2, 2, 2, 2, 1, 2, 2)
    weights = tuple(P("grp") if r == 1 else P("grp", None) for r in ranks)
    return jax.shard_map(
        partial(per_device, (mesh.shape["rep"], mesh.shape["grp"])),
        mesh=mesh,
        in_specs=(data3, data2, data3, data2, data3) + weights,
        out_specs=(data3, data3, data3) + weights,
        check_vma=False,
    )
```

```python
import math
from functools import partial
import jax
import jax.numpy as jnp
from jax import lax
from jax.sharding import PartitionSpec as P
from jax.experimental import pallas as pl
from jax.experimental.pallas import tpu as pltpu

HEADS = 14
HDIM = 64
STRETCH = 64
NEIGH = 2
NLEN = 128
BLOCK = 256
LANES = 128
EPS = 1e-06
NEG = -1000000000.0
SCALE = HDIM ** -0.5
F32 = jnp.float32
BF16 = jnp.bfloat16


def mm(a, b, ca, cb):
    return lax.dot_general(a, b, (((ca,), (cb,)), ((), ())), preferred_element_type=F32)


def low_lanes(shape):
    return lax.broadcasted_iota(jnp.int32, shape, len(shape) - 1) < HDIM


def self_fwd_kernel(q_ref, bc_ref, bp_ref, k_ref, v_ref, rel_ref, dr_ref, dc_ref, mixed_ref, *p_refs):
    length = k_ref.shape[0]
    query = q_ref[...]
    content_q = (query + bc_ref[...]).astype(BF16)
    position_q = (query + bp_ref[...]).astype(BF16)
    lo = low_lanes((1, LANES))
    masks = (lo, jnp.logical_not(lo))
    for index in range(length // BLOCK):
        first = index * BLOCK
        keys = first + BLOCK
        span = keys + BLOCK
        rel = rel_ref[length - keys : length - keys + span, :]
        cq = content_q[first:keys] * BF16(SCALE)
        pq = position_q[first:keys] * BF16(SCALE)
        same = dc_ref[0, first:keys, :] == dr_ref[0, :, :keys]
        outs = []
        for head in range(2):
            zero = jnp.zeros((), BF16)
            content = mm(jnp.where(masks[head], cq, zero), k_ref[:keys, :], 1, 1)
            full = mm(jnp.where(masks[head], pq, zero), rel, 1, 1)
            moved = pltpu.roll(full, span - BLOCK + 1, 1, stride=1, stride_axis=0)
            s = jnp.where(same, content + moved[:, :keys], NEG)
            e = jnp.exp(s - jnp.max(s, axis=1, keepdims=True))
            p = (e * (1.0 / jnp.sum(e, axis=1, keepdims=True))).astype(BF16)
            p_refs[index][0, 0, head] = p
            outs.append(mm(p, v_ref[:keys, :], 1, 0))
        mixed_ref[first:keys, :] = jnp.where(lo, outs[0], outs[1]).astype(BF16)


def self_bwd_kernel(q_ref, bc_ref, bp_ref, k_ref, v_ref, rel_ref, gm_ref, *refs):
    nblk = k_ref.shape[0] // BLOCK
    p_refs = refs[:nblk]
    gq_ref, gk_ref, gv_ref, grel_ref, gbc_ref, gbp_ref = refs[nblk : nblk + 6]
    gvt, gkt, grelt = refs[nblk + 6 :]
    length = k_ref.shape[0]
    seq = pl.program_id(1)
    query = q_ref[...]
    content_q = (query + bc_ref[...]).astype(BF16)
    position_q = (query + bp_ref[...]).astype(BF16)
    flip = (
        lax.broadcasted_iota(jnp.int32, (BLOCK, BLOCK), 0) + lax.broadcasted_iota(jnp.int32, (BLOCK, BLOCK), 1)
        == BLOCK - 1
    ).astype(BF16)
    gm = gm_ref[...]
    gmt = jnp.transpose(gm.astype(F32)).astype(BF16)
    lo = low_lanes((1, LANES))
    masks = (lo, jnp.logical_not(lo))
    zero = jnp.zeros((), BF16)
    gvt[...] = jnp.zeros_like(gvt)
    gkt[...] = jnp.zeros_like(gkt)
    grelt[...] = jnp.zeros_like(grelt)
    sum_c = jnp.zeros((1, LANES), F32)
    sum_p = jnp.zeros((1, LANES), F32)
    for index in range(nblk):
        first = index * BLOCK
        keys = first + BLOCK
        span = keys + BLOCK
        start = length - keys
        rel = rel_ref[start : start + span, :]
        gm_r = mm(flip, gm[first:keys], 1, 0).astype(BF16)
        cqt = jnp.transpose(mm(flip, content_q[first:keys] * BF16(SCALE), 1, 0)).astype(BF16)
        pqt = jnp.transpose(mm(flip, position_q[first:keys] * BF16(SCALE), 1, 0)).astype(BF16)
        gcs = []
        gps = []
        for head in range(2):
            hs = slice(head * HDIM, (head + 1) * HDIM)
            p = p_refs[index][0, 0, head]
            pf = mm(flip, p, 1, 0)
            g_p = mm(jnp.where(masks[head], gm_r, zero), v_ref[:keys, :], 1, 1)
            delta = jnp.sum(pf * g_p, axis=1, keepdims=True)
            gsf = pf * (g_p - delta)
            gs = gsf.astype(BF16)
            gvt[hs, :keys] += mm(gmt[hs, first:keys], p, 1, 0)
            gkt[hs, :keys] += mm(cqt[hs], gs, 1, 0)
            gcs.append(mm(gs, k_ref[:keys, :], 1, 0))
            padded = jnp.concatenate([gsf, jnp.zeros((BLOCK, BLOCK), F32)], axis=1)
            grel = pltpu.roll(padded, 0, 1, stride=1, stride_axis=0).astype(BF16)
            gps.append(mm(grel, rel, 1, 0))
            grelt[hs, start : start + span] += mm(pqt[hs], grel, 1, 0)
        gc = jnp.where(lo, gcs[0], gcs[1]) * SCALE
        gp = jnp.where(lo, gps[0], gps[1]) * SCALE
        sum_c += jnp.sum(gc, axis=0, keepdims=True)
        sum_p += jnp.sum(gp, axis=0, keepdims=True)
        gq_ref[first:keys, :] = mm(flip, (gc + gp).astype(BF16), 1, 0).astype(BF16)
    gv_ref[...] = jnp.transpose(gvt[...]).astype(BF16)
    gk_ref[...] = jnp.transpose(gkt[...]).astype(BF16)
    grel_ref[0] = jnp.transpose(grelt[...]).astype(BF16)

    @pl.when(seq == 0)
    def _():
        gbc_ref[...] = sum_c
        gbp_ref[...] = sum_p

    @pl.when(seq > 0)
    def _():
        gbc_ref[...] += sum_c
        gbp_ref[...] += sum_p


def self_specs(seqs, length, width):
    pairs = width // LANES
    table = length + BLOCK
    tok = pl.BlockSpec((length, LANES), lambda h, s: (s, h))
    vec = pl.BlockSpec((1, LANES), lambda h, s: (0, h))
    rel = pl.BlockSpec((table, LANES), lambda h, s: (0, h))
    probs = [
        pl.BlockSpec((1, 1, 2, BLOCK, (i + 1) * BLOCK), lambda h, s: (h, s, 0, 0, 0))
        for i in range(length // BLOCK)
    ]
    shapes = [
        jax.ShapeDtypeStruct((pairs, seqs, 2, BLOCK, (i + 1) * BLOCK), BF16)
        for i in range(length // BLOCK)
    ]
    return (pairs, seqs), tok, vec, rel, probs, shapes


def self_forward(query, bc, bp, key, value, rel_key, docs):
    seqs, length = docs.shape
    width = query.shape[1]
    grid, tok, vec, rel, pspecs, pshapes = self_specs(seqs, length, width)
    outs = pl.pallas_call(
        self_fwd_kernel,
        grid=grid,
        in_specs=[
            tok, vec, vec, tok, tok, rel,
            pl.BlockSpec((1, 1, length), lambda h, s: (s, 0, 0)),
            pl.BlockSpec((1, length, 1), lambda h, s: (s, 0, 0)),
        ],
        out_specs=[tok] + pspecs,
        out_shape=[jax.ShapeDtypeStruct(query.shape, BF16)] + pshapes,
        name="self_fwd",
    )(query, bc, bp, key, value, rel_key, docs[:, None, :], docs[:, :, None])
    return outs[0], outs[1:]


def self_backward(query, bc, bp, key, value, rel_key, g_mixed, probs):
    width = query.shape[1]
    seqs = probs[0].shape[1]
    length = query.shape[0] // seqs
    grid, tok, vec, rel, pspecs, _ = self_specs(seqs, length, width)
    table = length + BLOCK
    tshape = jax.ShapeDtypeStruct(query.shape, BF16)
    vshape = jax.ShapeDtypeStruct((1, width), F32)
    return pl.pallas_call(
        self_bwd_kernel,
        grid=grid,
        in_specs=[tok, vec, vec, tok, tok, rel, tok] + pspecs,
        out_specs=[tok, tok, tok, pl.BlockSpec((1, table, LANES), lambda h, s: (s, 0, h)), vec, vec],
        out_shape=[tshape, tshape, tshape, jax.ShapeDtypeStruct((seqs, table, width), BF16), vshape, vshape],
        scratch_shapes=[
            pltpu.VMEM((LANES, length), F32),
            pltpu.VMEM((LANES, length), F32),
            pltpu.VMEM((LANES, table), F32),
        ],
        name="self_bwd",
    )(query, bc, bp, key, value, rel_key, g_mixed, *probs)


def shift_up(v):
    return pltpu.roll(v, v.shape[0] - STRETCH + 1, 0)


def shift_down(v):
    moved = pltpu.roll(v, STRETCH - 1, 0)
    row = lax.broadcasted_iota(jnp.int32, (v.shape[0], 1), 0)
    return jnp.where(row >= STRETCH - 1, moved, 0.0)


def both_heads(v, lo):
    zero = jnp.zeros((), BF16)
    return jnp.concatenate([jnp.where(lo, v, zero), jnp.where(lo, zero, v)], axis=0)


def cross_fwd_kernel(rows_ref, q_ref, k0_ref, k1_ref, v0_ref, v1_ref, out_ref, p_ref, qs, os):
    u = pl.program_id(1)
    lo = low_lanes((1, LANES))

    @pl.when(u == 0)
    def _():
        qs[...] = shift_up(q_ref[...].astype(F32) * SCALE).astype(BF16)

    place = pl.ds(pl.multiple_of(u * STRETCH, STRETCH), STRETCH)
    for pair in range(q_ref.shape[1] // LANES):
        cols = slice(pair * LANES, (pair + 1) * LANES)
        q = both_heads(qs[place, cols], lo)
        k = jnp.concatenate([k0_ref[:, cols], k1_ref[:, cols]], axis=0)
        v = jnp.concatenate([v0_ref[:, cols], v1_ref[:, cols]], axis=0)
        s = mm(q, k, 1, 1)
        e = jnp.exp(s - jnp.max(s, axis=1, keepdims=True))
        p = (e * (1.0 / jnp.sum(e, axis=1, keepdims=True))).astype(BF16)
        p_ref[0, pair] = p
        o = mm(p, v, 1, 0)
        os[place, cols] = jnp.where(lo, o[:STRETCH], o[STRETCH:])

    @pl.when(u == pl.num_programs(1) - 1)
    def _():
        out_ref[...] = shift_down(os[...]).astype(BF16)


def cross_bwd_kernel(rows_ref, q_ref, g_ref, k0_ref, k1_ref, v0_ref, v1_ref, p_ref,
                     gq_ref, gk_ref, gv_ref, qs, gs_s, gq_s, gk_s, gv_s):
    u = pl.program_id(1)
    n = pl.program_id(2)
    lo = low_lanes((1, LANES))

    @pl.when(jnp.logical_and(u == 0, n == 0))
    def _():
        qs[...] = shift_up(q_ref[...].astype(F32) * SCALE).astype(BF16)
        g = g_ref[...].astype(F32)
        row = lax.broadcasted_iota(jnp.int32, (g.shape[0], 1), 0)
        gs_s[...] = shift_up(jnp.where(row >= STRETCH - 1, g, 0.0)).astype(BF16)

    @pl.when(n == 0)
    def _():
        place = pl.ds(pl.multiple_of(u * STRETCH, STRETCH), STRETCH)
        for pair in range(q_ref.shape[1] // LANES):
            cols = slice(pair * LANES, (pair + 1) * LANES)
            q = both_heads(qs[place, cols], lo)
            g = both_heads(gs_s[place, cols], lo)
            k = jnp.concatenate([k0_ref[:, cols], k1_ref[:, cols]], axis=0)
            v = jnp.concatenate([v0_ref[:, cols], v1_ref[:, cols]], axis=0)
            p = p_ref[0, pair]
            pf = p.astype(F32)
            g_p = mm(g, v, 1, 1)
            delta = jnp.sum(pf * g_p, axis=1, keepdims=True)
            gs = (pf * (g_p - delta)).astype(BF16)
            gv = mm(p, g, 0, 0).astype(BF16)
            gk = mm(gs, q, 0, 0).astype(BF16)
            gq = mm(gs, k, 1, 0)
            gq_s[place, cols] = jnp.where(lo, gq[:STRETCH], gq[STRETCH:]) * SCALE
            gk_ref[:, cols] = gk[:NLEN]
            gv_ref[:, cols] = gv[:NLEN]
            gk_s[:, cols] = gk[NLEN:]
            gv_s[:, cols] = gv[NLEN:]

    @pl.when(n == 1)
    def _():
        gk_ref[...] = gk_s[...]
        gv_ref[...] = gv_s[...]

    @pl.when(jnp.logical_and(u == pl.num_programs(1) - 1, n == 1))
    def _():
        gq_ref[...] = shift_down(gq_s[...]).astype(BF16)


def cross_forward(rows, cq, ck, cv, length):
    tokens, width = cq.shape
    seqs = tokens // length
    per = length // STRETCH
    pairs = width // LANES
    tok = pl.BlockSpec((length, width), lambda s, u, r: (s, 0))
    near = [
        pl.BlockSpec((NLEN, width), lambda s, u, r, n=n: (r[(s * per + u) * NEIGH + n], 0))
        for n in range(NEIGH)
    ]
    return pl.pallas_call(
        cross_fwd_kernel,
        grid_spec=pltpu.PrefetchScalarGridSpec(
            num_scalar_prefetch=1,
            grid=(seqs, per),
            in_specs=[tok] + near + near,
            out_specs=[
                tok,
                pl.BlockSpec((1, pairs, 2 * STRETCH, NEIGH * NLEN), lambda s, u, r: (s * per + u, 0, 0, 0)),
            ],
            scratch_shapes=[pltpu.VMEM((length, width), BF16), pltpu.VMEM((length, width), F32)],
        ),
        out_shape=[
            jax.ShapeDtypeStruct(cq.shape, BF16),
            jax.ShapeDtypeStruct((seqs * per, pairs, 2 * STRETCH, NEIGH * NLEN), BF16),
        ],
        name="cross_fwd",
    )(rows, cq, ck, ck, cv, cv)


def cross_backward(rows, cq, g_cmixed, ck, cv, probs, length):
    tokens, width = cq.shape
    seqs = tokens // length
    per = length // STRETCH
    pairs = width // LANES
    tok = pl.BlockSpec((length, width), lambda s, u, n, r: (s, 0))
    near = [
        pl.BlockSpec((NLEN, width), lambda s, u, n, r, m=m: (r[(s * per + u) * NEIGH + m], 0))
        for m in range(NEIGH)
    ]
    out = pl.BlockSpec((NLEN, width), lambda s, u, n, r: (r[(s * per + u) * NEIGH + n], 0))
    return pl.pallas_call(
        cross_bwd_kernel,
        grid_spec=pltpu.PrefetchScalarGridSpec(
            num_scalar_prefetch=1,
            grid=(seqs, per, NEIGH),
            in_specs=[tok, tok] + near + near + [
                pl.BlockSpec((1, pairs, 2 * STRETCH, NEIGH * NLEN), lambda s, u, n, r: (s * per + u, 0, 0, 0)),
            ],
            out_specs=[tok, out, out],
            scratch_shapes=[
                pltpu.VMEM((length, width), BF16),
                pltpu.VMEM((length, width), BF16),
                pltpu.VMEM((length, width), F32),
                pltpu.VMEM((NLEN, width), BF16),
                pltpu.VMEM((NLEN, width), BF16),
            ],
        ),
        out_shape=[
            jax.ShapeDtypeStruct(cq.shape, BF16),
            jax.ShapeDtypeStruct(ck.shape, BF16),
            jax.ShapeDtypeStruct(cv.shape, BF16),
        ],
        name="cross_bwd",
    )(rows, cq, g_cmixed, ck, ck, cv, cv, probs)


def lowered(v):
    return v.astype(BF16)


def norm_factor(v):
    return lax.rsqrt(jnp.mean(v * v, axis=-1, keepdims=True) + EPS)


def norm_back(v, gain, gy):
    r = norm_factor(v)
    part = gain * gy
    gain_part = jnp.sum(gy * v * r, axis=0)
    return r * part - v * (r * r * r) * jnp.mean(part * v, axis=-1, keepdims=True), gain_part


def position_table(length, width):
    column = jnp.arange(length + BLOCK, dtype=F32)
    distance = length - 1 - column
    rates = jnp.exp(jnp.arange(width // 2, dtype=F32) * (-2.0 * math.log(10000.0) / width))
    angles = distance[:, None] * rates[None, :]
    return jnp.concatenate([jnp.sin(angles), jnp.cos(angles)], axis=1)


SIDE = 8
CHIPS = 4
PARTS = 4
VECTORS = (0, 4, 5, 8, 13)
SINGLE = 12
SETS = ((1, 2, 3, 6), (10, 11, 7, 9), (14,), (15,))


def swap(v, bits):
    return lax.ppermute(v, "rep", [(r, r ^ bits) for r in range(SIDE)])


def shift(v, step):
    return lax.ppermute(v, "grp", [(g, (g + step) % PARTS) for g in range(PARTS)])


def total(parts):
    out = parts[0].astype(F32)
    for part in parts[1:]:
        out = out + part.astype(F32)
    return out


class Place:
    def __init__(self):
        me = lax.axis_index("rep")
        self.core = me % 2
        self.chip = me // 2
        self.grp = lax.axis_index("grp")
        self.table = jnp.stack(
            [jnp.bitwise_xor(self.chip, u) for u in range(CHIPS)]
            + [(self.grp + PARTS - s) % PARTS for s in range(PARTS)]
            + [self.core]
        ).astype(jnp.int32)


def assemble_kernel(kind, count, meta, *refs):
    locals_, mine, other, outs = refs[:count], refs[count], refs[count + 1], refs[count + 2 :]
    high = mine.shape[2]
    here = meta[CHIPS]
    core = meta[CHIPS + PARTS]
    for i in range(count):
        rows = locals_[i].shape[0]
        outs[i][pl.ds(pl.multiple_of(here * rows, 16), rows), :] = locals_[i][...]
    units = 1 if kind in ("up", "one") else CHIPS
    for u in range(units):
        src = meta[u] if units > 1 else 0
        for s in range(1, PARTS):
            k = meta[CHIPS + s]
            for ref, half in ((mine, core), (other, 1 - core)):
                row = k * 2 * high + half * high
                if kind == "down":
                    row = k * CHIPS * 2 * high + u * 2 * high + half * high
                out = outs[u] if kind == "four" else outs[0]
                out[pl.ds(pl.multiple_of(row, 16), high), :] = ref[src, s - 1]


def assemble(kind, place, locals_, mine, other):
    units, steps, high, width = mine.shape
    count = len(locals_)
    cols = width // LANES
    if kind == "up":
        grid = (CHIPS, cols)
        piece = pl.BlockSpec((1, steps, high, LANES), lambda u, j, m: (m[u], 0, 0, j))
        place_of = lambda u, j, m: (0, u * cols + j)
    else:
        grid = (cols,)
        piece = pl.BlockSpec((units, steps, high, LANES), lambda j, m: (0, 0, 0, j))
        place_of = lambda j, m: (0, j)
    shapes = [jax.ShapeDtypeStruct((PARTS * a.shape[0], a.shape[1]), a.dtype) for a in locals_]
    return pl.pallas_call(
        partial(assemble_kernel, kind, count),
        grid_spec=pltpu.PrefetchScalarGridSpec(
            num_scalar_prefetch=1,
            grid=grid,
            in_specs=[pl.BlockSpec((a.shape[0], LANES), place_of) for a in locals_] + [piece, piece],
            out_specs=[pl.BlockSpec((s.shape[0], LANES), place_of) for s in shapes],
        ),
        out_shape=shapes,
        cost_estimate=pl.CostEstimate(flops=0, transcendentals=0, bytes_accessed=sum(4 * s.shape[0] * s.shape[1] for s in shapes)),
        name="assemble_" + kind,
    )(place.table, *locals_, mine, other)


def pick(parts, index):
    out = parts[0]
    for n in range(1, len(parts)):
        out = jnp.where(index == n, parts[n], out)
    return out


def set_kind(members, local):
    if len(members) > 1:
        return "four"
    return "up" if local[members[0]].shape[1] > local[members[0]].shape[0] else "down"


def own_piece(kind, place, locals_):
    if kind == "four":
        high = locals_[0].shape[0] // 2
        return pick([lax.dynamic_slice_in_dim(a, place.core * high, high, 0) for a in locals_], place.chip)
    a = locals_[0]
    if kind == "down":
        high = a.shape[0] // SIDE
        return lax.dynamic_slice_in_dim(a, (place.chip * 2 + place.core) * high, high, 0)
    high, width = a.shape[0] // 2, a.shape[1] // CHIPS
    return lax.dynamic_slice(a, (place.core * high, place.chip * width), (high, width))


def tie(*values):
    return lax.optimization_barrier(values)


def gather_vectors(place, local):
    small = jnp.stack([local[i] for i in VECTORS])
    slots = jnp.stack([small] + [shift(small, s) for s in range(1, PARTS)])
    order = [lax.dynamic_index_in_dim(slots, (place.grp + PARTS - k) % PARTS, 0, keepdims=False) for k in range(PARTS)]
    return jnp.concatenate(order, axis=1)


class Gather:
    def __init__(self, place, local, members):
        self.place = place
        self.members = members
        self.locals_ = [local[i] for i in members]
        self.kind = "one" if members == (SINGLE,) else set_kind(members, local)
        if self.kind == "one":
            high = self.locals_[0].shape[0] // 2
            self.own = lax.dynamic_slice_in_dim(self.locals_[0], place.core * high, high, 0)
        else:
            self.own = own_piece(self.kind, place, self.locals_)

    def along_grp(self):
        self.got = jnp.stack([shift(self.own, s) for s in range(1, PARTS)])

    def in_plane(self):
        if self.kind == "one":
            self.mine = self.got[None]
        else:
            self.mine = jnp.stack([self.got] + [swap(self.got, 2 * b) for b in range(1, CHIPS)])

    def between_cores(self):
        self.other = swap(self.mine, 1)

    def finish(self, full):
        for i, w in zip(self.members, assemble(self.kind, self.place, self.locals_, self.mine, self.other)):
            full[i] = w


def spread_kernel(meta, *refs):
    half = len(refs) // 2
    for n in range(half):
        refs[half + n][...] = refs[n][0, 0].astype(F32)


def spread(kind, place, stack, shapes):
    high, width = stack.shape[2:]
    block = (1, 1, high, width)
    if kind == "four":
        grid = (2,)
        ins = [pl.BlockSpec(block, lambda h, m, u=u: (m[u], jnp.bitwise_xor(h, m[CHIPS + PARTS]), 0, 0)) for u in range(CHIPS)]
        outs = [pl.BlockSpec((high, width), lambda h, m: (h, 0))] * CHIPS
    else:
        grid = (CHIPS, 2)
        ins = [pl.BlockSpec(block, lambda u, h, m: (m[u], jnp.bitwise_xor(h, m[CHIPS + PARTS]), 0, 0))]
        if kind == "down":
            outs = [pl.BlockSpec((high, width), lambda u, h, m: (2 * u + h, 0))]
        else:
            outs = [pl.BlockSpec((high, width), lambda u, h, m: (h, u))]
    return pl.pallas_call(
        spread_kernel,
        grid_spec=pltpu.PrefetchScalarGridSpec(num_scalar_prefetch=1, grid=grid, in_specs=ins, out_specs=outs),
        out_shape=[jax.ShapeDtypeStruct(s, F32) for s in shapes],
        name="spread_" + kind,
    )(place.table, *([stack] * len(ins)))


def grad_piece(kind, place, grads, unit, half):
    if kind == "four":
        a = grads[0]
        high = a.shape[3]
        out = lax.dynamic_slice(a, (unit, 0, half, 0, 0), (1, PARTS, 1, high, a.shape[4]))
        return out.reshape(PARTS, high, a.shape[4])
    rows, cols = grads[0].shape
    if kind == "down":
        high = rows // (PARTS * SIDE)
        a = grads[0].reshape(PARTS, SIDE, high, cols)
        return lax.dynamic_index_in_dim(a, 2 * unit + half, 1, keepdims=False)
    high, width = rows // (PARTS * 2), cols // CHIPS
    a = grads[0].reshape(PARTS, 2, high, cols)
    out = lax.dynamic_slice(a, (0, half, 0, unit * width), (PARTS, 1, high, width))
    return out.reshape(PARTS, high, width)


def scatter_grp(place, parts):
    send = [lax.dynamic_index_in_dim(parts, (place.grp + s) % PARTS, 0, keepdims=False) for s in range(PARTS)]
    return total([send[0]] + [shift(send[s], s) for s in range(1, PARTS)])


class Reduce:
    def __init__(self, place, kind, grads, shapes):
        self.place, self.kind, self.shapes = place, kind, shapes
        if kind == "four":
            rows, cols = grads[0].shape
            grads = [jnp.stack(grads).reshape(CHIPS, PARTS, 2, rows // (2 * PARTS), cols)]
        self.grads = grads
        self.units = [jnp.bitwise_xor(place.chip, b) for b in range(CHIPS)]
        self.send = jnp.stack([grad_piece(kind, place, grads, u, 1 - place.core) for u in self.units])

    def between_cores(self):
        got = swap(self.send, 1)
        self.sums = tuple(
            lowered(total([grad_piece(self.kind, self.place, self.grads, u, self.place.core), got[b]]))
            for b, u in enumerate(self.units)
        )

    def in_plane(self):
        self.part = lowered(total([self.sums[0]] + [swap(self.sums[b], 2 * b) for b in range(1, CHIPS)]))

    def along_grp(self):
        self.mine = lowered(scatter_grp(self.place, self.part))

    def back_plane(self):
        self.all = jnp.stack([self.mine] + [swap(self.mine, 2 * b) for b in range(1, CHIPS)])

    def finish(self):
        other = swap(self.all, 1)
        return spread(self.kind, self.place, jnp.stack([self.all, other], axis=1), self.shapes)


def reduce_single(place, grad):
    rows, cols = grad.shape
    a = grad.reshape(PARTS, 2, rows // (2 * PARTS), cols)
    got = swap(lax.dynamic_index_in_dim(a, 1 - place.core, 1, keepdims=False), 1)
    part = lowered(total([lax.dynamic_index_in_dim(a, place.core, 1, keepdims=False), got]))
    mine = lowered(scatter_grp(place, part))
    mine = lowered(total([mine] + [swap(mine, 2 * b) for b in range(1, CHIPS)]))
    other = swap(mine, 1)
    first = jnp.where(place.core == 0, mine, other)
    second = jnp.where(place.core == 0, other, mine)
    return jnp.concatenate([first, second], axis=0).astype(F32)


def reduce_vectors(place, small):
    for bits in (1, 2, 4):
        small = small + swap(small, bits)
    for bits in (1, 2):
        small = small + lax.ppermute(small, "grp", [(g, g ^ bits) for g in range(PARTS)])
    piece = small.shape[1] // PARTS
    return lax.dynamic_slice_in_dim(small, place.grp * piece, piece, axis=1)


def per_device(mesh_shape, tokens, docs, neighbours, neighbour_rows, out_grad, *local):
    reps, groups = mesh_shape
    fast = reps == SIDE and groups == PARTS
    rows = neighbour_rows.reshape(-1) % neighbours.shape[0]
    seqs, length, width = tokens.shape
    count = seqs * length
    near = neighbours.reshape(-1, width)
    table = lowered(position_table(length, width))
    x = tokens.reshape(count, width).astype(F32)
    full = [None] * len(local)
    place = Place()
    if fast:
        vectors = gather_vectors(place, local)
        for n, i in enumerate(VECTORS):
            full[i] = vectors[n]
        sets = [Gather(place, local, m) for m in SETS]
        single = Gather(place, local, (SINGLE,))
        sets[0].along_grp()
        sets[1].own, sets[0].got = tie(sets[1].own, sets[0].got)
        sets[0].in_plane()
        sets[1].along_grp()
        sets[2].own, sets[1].got, sets[0].mine = tie(sets[2].own, sets[1].got, sets[0].mine)
        sets[0].between_cores()
        sets[1].in_plane()
        sets[2].along_grp()
        sets[0].finish(full)
        single.own, sets[3].own, sets[2].got, full[1] = tie(single.own, sets[3].own, sets[2].got, full[1])
        sets[2].in_plane()
        single.along_grp()
        sets[3].along_grp()
    else:
        full = [lax.all_gather(a, "grp", axis=0, tiled=True) for a in local]
    ag, bc, bp, cg, fg = (full[i].astype(F32) for i in VECTORS)
    bc, bp = bc[None], bp[None]
    normed = lowered(x * norm_factor(x) * ag)
    query = mm(normed, full[1], 1, 0)
    key = lowered(mm(normed, full[2], 1, 0))
    value = lowered(mm(normed, full[3], 1, 0))
    rel_key = lowered(mm(table, full[6], 1, 0))
    mixed, probs = self_forward(query, bc, bp, key, value, rel_key, docs)
    if fast:
        mixed, sets[1].mine, sets[2].mine, sets[3].got, single.got = tie(
            mixed, sets[1].mine, sets[2].mine, sets[3].got, single.got
        )
        sets[1].between_cores()
        sets[3].in_plane()
        single.in_plane()
        single.between_cores()
        sets[2].between_cores()
        sets[1].finish(full)
    ck = lowered(mm(near, full[10], 1, 0))
    cv = lowered(mm(near, full[11], 1, 0))
    if fast:
        ck, cv, sets[2].other, single.other, mixed = tie(ck, cv, sets[2].other, single.other, mixed)
    hidden = x + mm(mixed, full[7], 1, 0)
    cnorm = lowered(hidden * norm_factor(hidden) * cg)
    cq = lowered(mm(cnorm, full[9], 1, 0))
    if fast:
        cq, sets[3].mine = tie(cq, sets[3].mine)
        sets[3].between_cores()
    cmixed, cprobs = cross_forward(rows, cq, ck, cv, length)
    if fast:
        cmixed, sets[3].other, sets[2].other = tie(cmixed, sets[3].other, sets[2].other)
        single.finish(full)
        sets[2].finish(full)
        sets[3].finish(full)
    hidden2 = hidden + mm(cmixed, full[12], 1, 0)
    fnorm = lowered(hidden2 * norm_factor(hidden2) * fg)
    upper = mm(fnorm, full[14], 1, 0)
    active = lowered(jax.nn.gelu(upper))
    result = lowered(hidden2 + mm(active, full[15], 1, 0))

    gy = out_grad.reshape(count, width)
    g_down = lowered(mm(active, gy, 0, 0))
    if fast:
        r_down = Reduce(place, "down", [g_down], [local[15].shape])
        gy, r_down.send, result = tie(gy, r_down.send, result)
    g_active = mm(gy, full[15], 1, 1)
    g_upper = lowered(jax.vjp(jax.nn.gelu, upper)[1](g_active)[0])
    g_up = lowered(mm(fnorm, g_upper, 0, 0))
    if fast:
        r_down.between_cores()
        r_up = Reduce(place, "up", [g_up], [local[14].shape])
        g_upper, r_up.send, r_down.sums = tie(g_upper, r_up.send, r_down.sums)
        r_down.in_plane()
    g_fnorm = mm(g_upper, full[14], 1, 1)
    part, g_fg = norm_back(hidden2, fg, g_fnorm)
    g_h2 = gy.astype(F32) + part
    g_branch = lowered(g_h2)
    g_cproj = lowered(mm(cmixed, g_branch, 0, 0))
    g_cmixed = lowered(mm(g_branch, full[12], 1, 1))
    if fast:
        r_up.between_cores()
        g_cmixed, r_up.sums = tie(g_cmixed, r_up.sums)
        r_up.in_plane()
    g_cq, g_ck, g_cv = cross_backward(rows, cq, g_cmixed, ck, cv, cprobs, length)
    if fast:
        g_cq, r_down.part, r_up.part = tie(g_cq, r_down.part, r_up.part)
        r_down.along_grp()
        r_up.along_grp()
    g_cquery_w = lowered(mm(cnorm, g_cq, 0, 0))
    g_ckey_w = lowered(mm(near, g_ck, 0, 0))
    g_cvalue_w = lowered(mm(near, g_cv, 0, 0))
    g_cnorm = mm(g_cq, full[9], 1, 1)
    part, g_cg = norm_back(hidden, cg, g_cnorm)
    g_h1 = g_h2 + part
    g_attn = lowered(g_h1)
    g_aproj = lowered(mm(mixed, g_attn, 0, 0))
    if fast:
        r_cross = Reduce(place, "four", [g_ckey_w, g_cvalue_w, g_aproj, g_cquery_w], [local[10].shape] * CHIPS)
        g_attn, r_cross.send = tie(g_attn, r_cross.send)
    g_near = lowered(mm(g_ck, full[10], 1, 1) + mm(g_cv, full[11], 1, 1)).reshape(neighbours.shape)
    g_mixed = lowered(mm(g_attn, full[7], 1, 1))
    if fast:
        r_cross.between_cores()
        g_mixed, g_near, r_cross.sums, r_down.mine, r_up.mine = tie(g_mixed, g_near, r_cross.sums, r_down.mine, r_up.mine)
        r_cross.in_plane()
        r_down.back_plane()
        r_up.back_plane()
    g_q, g_k, g_v, g_relk, g_bc, g_bp = self_backward(query, bc, bp, key, value, rel_key, g_mixed, probs)
    if fast:
        g_q, g_k, g_v, r_cross.part, r_down.all, r_up.all = tie(g_q, g_k, g_v, r_cross.part, r_down.all, r_up.all)
        r_cross.along_grp()
    g_rel_sum = lowered(jnp.sum(g_relk.astype(F32), axis=0))
    g_rel = lowered(mm(table, g_rel_sum, 0, 0))
    g_query_w = lowered(mm(normed, g_q, 0, 0))
    g_key_w = lowered(mm(normed, g_k, 0, 0))
    g_value_w = lowered(mm(normed, g_v, 0, 0))
    if fast:
        r_self = Reduce(place, "four", [g_query_w, g_key_w, g_value_w, g_rel], [local[1].shape] * CHIPS)
        g_q, g_k, g_v, r_self.send = tie(g_q, g_k, g_v, r_self.send)
        r_self.between_cores()
    g_normed = mm(g_q, full[1], 1, 1) + mm(g_k, full[2], 1, 1) + mm(g_v, full[3], 1, 1)
    part, g_ag = norm_back(x, ag, g_normed)
    grad_x = lowered(g_h1 + part)
    small = [g_ag, g_bc[0], g_bp[0], g_cg, g_fg]
    out = [None] * len(local)
    if fast:
        r_self.in_plane()
        r_self.along_grp()
        r_self.back_plane()
        r_cross.back_plane()
        vectors = reduce_vectors(place, jnp.stack(small))
        for n, i in enumerate(VECTORS):
            out[i] = vectors[n]
        out[SINGLE] = reduce_single(place, g_cproj)
        out[15] = r_down.finish()[0]
        out[14] = r_up.finish()[0]
        for i, w in zip((10, 11, 7, 9), r_cross.finish()):
            out[i] = w
        for i, w in zip((1, 2, 3, 6), r_self.finish()):
            out[i] = w
    else:
        grads = [None, g_query_w, g_key_w, g_value_w, None, None, g_rel, g_aproj, None, g_cquery_w, g_ckey_w,
                 g_cvalue_w, g_cproj, None, g_up, g_down]
        for n, i in enumerate(VECTORS):
            grads[i] = small[n]
        for i, g in enumerate(grads):
            shard = lax.psum_scatter(lowered(g), "grp", scatter_dimension=0, tiled=True)
            out[i] = lax.psum(shard.astype(F32), "rep")
    return (result.reshape(tokens.shape), grad_x.reshape(tokens.shape), g_near) + tuple(out)


def solution(mesh):
    data3 = P(("rep", "grp"), None, None)
    data2 = P(("rep", "grp"), None)
    ranks = (1, 2, 2, 2, 1, 1, 2, 2, 1, 2, 2, 2, 2, 1, 2, 2)
    weights = tuple(P("grp") if r == 1 else P("grp", None) for r in ranks)
    return jax.shard_map(
        partial(per_device, (mesh.shape["rep"], mesh.shape["grp"])),
        mesh=mesh,
        in_specs=(data3, data2, data3, data2, data3) + weights,
        out_specs=(data3, data3, data3) + weights,
        check_vma=False,
    )
```

```python
import math
from functools import partial
import jax
import jax.numpy as jnp
from jax import lax
from jax.sharding import PartitionSpec as P
from jax.experimental import pallas as pl
from jax.experimental.pallas import tpu as pltpu

HEADS = 14
HDIM = 64
STRETCH = 64
NEIGH = 2
NLEN = 128
BLOCK = 256
LANES = 128
EPS = 1e-06
NEG = -1000000000.0
SCALE = HDIM ** -0.5
F32 = jnp.float32
BF16 = jnp.bfloat16


def mm(a, b, ca, cb):
    return lax.dot_general(a, b, (((ca,), (cb,)), ((), ())), preferred_element_type=F32)


def low_lanes(shape):
    return lax.broadcasted_iota(jnp.int32, shape, len(shape) - 1) < HDIM


def self_fwd_kernel(q_ref, bc_ref, bp_ref, k_ref, v_ref, rel_ref, dr_ref, dc_ref, mixed_ref, *p_refs):
    length = k_ref.shape[0]
    query = q_ref[...]
    content_q = (query + bc_ref[...]).astype(BF16)
    position_q = (query + bp_ref[...]).astype(BF16)
    lo = low_lanes((1, LANES))
    masks = (lo, jnp.logical_not(lo))
    for index in range(length // BLOCK):
        first = index * BLOCK
        keys = first + BLOCK
        span = keys + BLOCK
        rel = rel_ref[length - keys : length - keys + span, :]
        cq = content_q[first:keys] * BF16(SCALE)
        pq = position_q[first:keys] * BF16(SCALE)
        same = dc_ref[0, first:keys, :] == dr_ref[0, :, :keys]
        outs = []
        for head in range(2):
            zero = jnp.zeros((), BF16)
            content = mm(jnp.where(masks[head], cq, zero), k_ref[:keys, :], 1, 1)
            full = mm(jnp.where(masks[head], pq, zero), rel, 1, 1)
            moved = pltpu.roll(full, span - BLOCK + 1, 1, stride=1, stride_axis=0)
            s = jnp.where(same, content + moved[:, :keys], NEG)
            e = jnp.exp(s - jnp.max(s, axis=1, keepdims=True))
            p = (e * (1.0 / jnp.sum(e, axis=1, keepdims=True))).astype(BF16)
            p_refs[index][0, 0, head] = p
            outs.append(mm(p, v_ref[:keys, :], 1, 0))
        mixed_ref[first:keys, :] = jnp.where(lo, outs[0], outs[1]).astype(BF16)


def self_bwd_kernel(q_ref, bc_ref, bp_ref, k_ref, v_ref, rel_ref, gm_ref, *refs):
    nblk = k_ref.shape[0] // BLOCK
    p_refs = refs[:nblk]
    gq_ref, gk_ref, gv_ref, grel_ref, gbc_ref, gbp_ref = refs[nblk : nblk + 6]
    gvt, gkt, grelt = refs[nblk + 6 :]
    length = k_ref.shape[0]
    seq = pl.program_id(1)
    query = q_ref[...]
    content_q = (query + bc_ref[...]).astype(BF16)
    position_q = (query + bp_ref[...]).astype(BF16)
    flip = (
        lax.broadcasted_iota(jnp.int32, (BLOCK, BLOCK), 0) + lax.broadcasted_iota(jnp.int32, (BLOCK, BLOCK), 1)
        == BLOCK - 1
    ).astype(BF16)
    gm = gm_ref[...]
    gmt = jnp.transpose(gm.astype(F32)).astype(BF16)
    lo = low_lanes((1, LANES))
    masks = (lo, jnp.logical_not(lo))
    zero = jnp.zeros((), BF16)
    gvt[...] = jnp.zeros_like(gvt)
    gkt[...] = jnp.zeros_like(gkt)
    grelt[...] = jnp.zeros_like(grelt)
    sum_c = jnp.zeros((1, LANES), F32)
    sum_p = jnp.zeros((1, LANES), F32)
    for index in range(nblk):
        first = index * BLOCK
        keys = first + BLOCK
        span = keys + BLOCK
        start = length - keys
        rel = rel_ref[start : start + span, :]
        gm_r = mm(flip, gm[first:keys], 1, 0).astype(BF16)
        cqt = jnp.transpose(mm(flip, content_q[first:keys] * BF16(SCALE), 1, 0)).astype(BF16)
        pqt = jnp.transpose(mm(flip, position_q[first:keys] * BF16(SCALE), 1, 0)).astype(BF16)
        gcs = []
        gps = []
        for head in range(2):
            hs = slice(head * HDIM, (head + 1) * HDIM)
            p = p_refs[index][0, 0, head]
            pf = mm(flip, p, 1, 0)
            g_p = mm(jnp.where(masks[head], gm_r, zero), v_ref[:keys, :], 1, 1)
            delta = jnp.sum(pf * g_p, axis=1, keepdims=True)
            gsf = pf * (g_p - delta)
            gs = gsf.astype(BF16)
            gvt[hs, :keys] += mm(gmt[hs, first:keys], p, 1, 0)
            gkt[hs, :keys] += mm(cqt[hs], gs, 1, 0)
            gcs.append(mm(gs, k_ref[:keys, :], 1, 0))
            padded = jnp.concatenate([gsf, jnp.zeros((BLOCK, BLOCK), F32)], axis=1)
            grel = pltpu.roll(padded, 0, 1, stride=1, stride_axis=0).astype(BF16)
            gps.append(mm(grel, rel, 1, 0))
            grelt[hs, start : start + span] += mm(pqt[hs], grel, 1, 0)
        gc = jnp.where(lo, gcs[0], gcs[1]) * SCALE
        gp = jnp.where(lo, gps[0], gps[1]) * SCALE
        sum_c += jnp.sum(gc, axis=0, keepdims=True)
        sum_p += jnp.sum(gp, axis=0, keepdims=True)
        gq_ref[first:keys, :] = mm(flip, (gc + gp).astype(BF16), 1, 0).astype(BF16)
    gv_ref[...] = jnp.transpose(gvt[...]).astype(BF16)
    gk_ref[...] = jnp.transpose(gkt[...]).astype(BF16)
    grel_ref[0] = jnp.transpose(grelt[...]).astype(BF16)

    @pl.when(seq == 0)
    def _():
        gbc_ref[...] = sum_c
        gbp_ref[...] = sum_p

    @pl.when(seq > 0)
    def _():
        gbc_ref[...] += sum_c
        gbp_ref[...] += sum_p


def self_specs(seqs, length, width):
    pairs = width // LANES
    table = length + BLOCK
    tok = pl.BlockSpec((length, LANES), lambda h, s: (s, h))
    vec = pl.BlockSpec((1, LANES), lambda h, s: (0, h))
    rel = pl.BlockSpec((table, LANES), lambda h, s: (0, h))
    probs = [
        pl.BlockSpec((1, 1, 2, BLOCK, (i + 1) * BLOCK), lambda h, s: (h, s, 0, 0, 0))
        for i in range(length // BLOCK)
    ]
    shapes = [
        jax.ShapeDtypeStruct((pairs, seqs, 2, BLOCK, (i + 1) * BLOCK), BF16)
        for i in range(length // BLOCK)
    ]
    return (pairs, seqs), tok, vec, rel, probs, shapes


def self_forward(query, bc, bp, key, value, rel_key, docs):
    seqs, length = docs.shape
    width = query.shape[1]
    grid, tok, vec, rel, pspecs, pshapes = self_specs(seqs, length, width)
    outs = pl.pallas_call(
        self_fwd_kernel,
        grid=grid,
        in_specs=[
            tok, vec, vec, tok, tok, rel,
            pl.BlockSpec((1, 1, length), lambda h, s: (s, 0, 0)),
            pl.BlockSpec((1, length, 1), lambda h, s: (s, 0, 0)),
        ],
        out_specs=[tok] + pspecs,
        out_shape=[jax.ShapeDtypeStruct(query.shape, BF16)] + pshapes,
        name="self_fwd",
    )(query, bc, bp, key, value, rel_key, docs[:, None, :], docs[:, :, None])
    return outs[0], outs[1:]


def self_backward(query, bc, bp, key, value, rel_key, g_mixed, probs):
    width = query.shape[1]
    seqs = probs[0].shape[1]
    length = query.shape[0] // seqs
    grid, tok, vec, rel, pspecs, _ = self_specs(seqs, length, width)
    table = length + BLOCK
    tshape = jax.ShapeDtypeStruct(query.shape, BF16)
    vshape = jax.ShapeDtypeStruct((1, width), F32)
    return pl.pallas_call(
        self_bwd_kernel,
        grid=grid,
        in_specs=[tok, vec, vec, tok, tok, rel, tok] + pspecs,
        out_specs=[tok, tok, tok, pl.BlockSpec((1, table, LANES), lambda h, s: (s, 0, h)), vec, vec],
        out_shape=[tshape, tshape, tshape, jax.ShapeDtypeStruct((seqs, table, width), BF16), vshape, vshape],
        scratch_shapes=[
            pltpu.VMEM((LANES, length), F32),
            pltpu.VMEM((LANES, length), F32),
            pltpu.VMEM((LANES, table), F32),
        ],
        name="self_bwd",
    )(query, bc, bp, key, value, rel_key, g_mixed, *probs)


def shift_up(v):
    return pltpu.roll(v, v.shape[0] - STRETCH + 1, 0)


def shift_down(v):
    moved = pltpu.roll(v, STRETCH - 1, 0)
    row = lax.broadcasted_iota(jnp.int32, (v.shape[0], 1), 0)
    return jnp.where(row >= STRETCH - 1, moved, 0.0)


def both_heads(v, lo):
    zero = jnp.zeros((), BF16)
    return jnp.concatenate([jnp.where(lo, v, zero), jnp.where(lo, zero, v)], axis=0)


def cross_fwd_kernel(rows_ref, q_ref, k0_ref, k1_ref, v0_ref, v1_ref, out_ref, p_ref, qs, os):
    u = pl.program_id(1)
    lo = low_lanes((1, LANES))

    @pl.when(u == 0)
    def _():
        qs[...] = shift_up(q_ref[...].astype(F32) * SCALE).astype(BF16)

    place = pl.ds(pl.multiple_of(u * STRETCH, STRETCH), STRETCH)
    for pair in range(q_ref.shape[1] // LANES):
        cols = slice(pair * LANES, (pair + 1) * LANES)
        q = both_heads(qs[place, cols], lo)
        k = jnp.concatenate([k0_ref[:, cols], k1_ref[:, cols]], axis=0)
        v = jnp.concatenate([v0_ref[:, cols], v1_ref[:, cols]], axis=0)
        s = mm(q, k, 1, 1)
        e = jnp.exp(s - jnp.max(s, axis=1, keepdims=True))
        p = (e * (1.0 / jnp.sum(e, axis=1, keepdims=True))).astype(BF16)
        p_ref[0, pair] = p
        o = mm(p, v, 1, 0)
        os[place, cols] = jnp.where(lo, o[:STRETCH], o[STRETCH:])

    @pl.when(u == pl.num_programs(1) - 1)
    def _():
        out_ref[...] = shift_down(os[...]).astype(BF16)


def cross_bwd_kernel(rows_ref, q_ref, g_ref, k0_ref, k1_ref, v0_ref, v1_ref, p_ref,
                     gq_ref, gk_ref, gv_ref, qs, gs_s, gq_s, gk_s, gv_s):
    u = pl.program_id(1)
    n = pl.program_id(2)
    lo = low_lanes((1, LANES))

    @pl.when(jnp.logical_and(u == 0, n == 0))
    def _():
        qs[...] = shift_up(q_ref[...].astype(F32) * SCALE).astype(BF16)
        g = g_ref[...].astype(F32)
        row = lax.broadcasted_iota(jnp.int32, (g.shape[0], 1), 0)
        gs_s[...] = shift_up(jnp.where(row >= STRETCH - 1, g, 0.0)).astype(BF16)

    @pl.when(n == 0)
    def _():
        place = pl.ds(pl.multiple_of(u * STRETCH, STRETCH), STRETCH)
        for pair in range(q_ref.shape[1] // LANES):
            cols = slice(pair * LANES, (pair + 1) * LANES)
            q = both_heads(qs[place, cols], lo)
            g = both_heads(gs_s[place, cols], lo)
            k = jnp.concatenate([k0_ref[:, cols], k1_ref[:, cols]], axis=0)
            v = jnp.concatenate([v0_ref[:, cols], v1_ref[:, cols]], axis=0)
            p = p_ref[0, pair]
            pf = p.astype(F32)
            g_p = mm(g, v, 1, 1)
            delta = jnp.sum(pf * g_p, axis=1, keepdims=True)
            gs = (pf * (g_p - delta)).astype(BF16)
            gv = mm(p, g, 0, 0).astype(BF16)
            gk = mm(gs, q, 0, 0).astype(BF16)
            gq = mm(gs, k, 1, 0)
            gq_s[place, cols] = jnp.where(lo, gq[:STRETCH], gq[STRETCH:]) * SCALE
            gk_ref[:, cols] = gk[:NLEN]
            gv_ref[:, cols] = gv[:NLEN]
            gk_s[:, cols] = gk[NLEN:]
            gv_s[:, cols] = gv[NLEN:]

    @pl.when(n == 1)
    def _():
        gk_ref[...] = gk_s[...]
        gv_ref[...] = gv_s[...]

    @pl.when(jnp.logical_and(u == pl.num_programs(1) - 1, n == 1))
    def _():
        gq_ref[...] = shift_down(gq_s[...]).astype(BF16)


def cross_forward(rows, cq, ck, cv, length):
    tokens, width = cq.shape
    seqs = tokens // length
    per = length // STRETCH
    pairs = width // LANES
    tok = pl.BlockSpec((length, width), lambda s, u, r: (s, 0))
    near = [
        pl.BlockSpec((NLEN, width), lambda s, u, r, n=n: (r[(s * per + u) * NEIGH + n], 0))
        for n in range(NEIGH)
    ]
    return pl.pallas_call(
        cross_fwd_kernel,
        grid_spec=pltpu.PrefetchScalarGridSpec(
            num_scalar_prefetch=1,
            grid=(seqs, per),
            in_specs=[tok] + near + near,
            out_specs=[
                tok,
                pl.BlockSpec((1, pairs, 2 * STRETCH, NEIGH * NLEN), lambda s, u, r: (s * per + u, 0, 0, 0)),
            ],
            scratch_shapes=[pltpu.VMEM((length, width), BF16), pltpu.VMEM((length, width), F32)],
        ),
        out_shape=[
            jax.ShapeDtypeStruct(cq.shape, BF16),
            jax.ShapeDtypeStruct((seqs * per, pairs, 2 * STRETCH, NEIGH * NLEN), BF16),
        ],
        name="cross_fwd",
    )(rows, cq, ck, ck, cv, cv)


def cross_backward(rows, cq, g_cmixed, ck, cv, probs, length):
    tokens, width = cq.shape
    seqs = tokens // length
    per = length // STRETCH
    pairs = width // LANES
    tok = pl.BlockSpec((length, width), lambda s, u, n, r: (s, 0))
    near = [
        pl.BlockSpec((NLEN, width), lambda s, u, n, r, m=m: (r[(s * per + u) * NEIGH + m], 0))
        for m in range(NEIGH)
    ]
    out = pl.BlockSpec((NLEN, width), lambda s, u, n, r: (r[(s * per + u) * NEIGH + n], 0))
    return pl.pallas_call(
        cross_bwd_kernel,
        grid_spec=pltpu.PrefetchScalarGridSpec(
            num_scalar_prefetch=1,
            grid=(seqs, per, NEIGH),
            in_specs=[tok, tok] + near + near + [
                pl.BlockSpec((1, pairs, 2 * STRETCH, NEIGH * NLEN), lambda s, u, n, r: (s * per + u, 0, 0, 0)),
            ],
            out_specs=[tok, out, out],
            scratch_shapes=[
                pltpu.VMEM((length, width), BF16),
                pltpu.VMEM((length, width), BF16),
                pltpu.VMEM((length, width), F32),
                pltpu.VMEM((NLEN, width), BF16),
                pltpu.VMEM((NLEN, width), BF16),
            ],
        ),
        out_shape=[
            jax.ShapeDtypeStruct(cq.shape, BF16),
            jax.ShapeDtypeStruct(ck.shape, BF16),
            jax.ShapeDtypeStruct(cv.shape, BF16),
        ],
        name="cross_bwd",
    )(rows, cq, g_cmixed, ck, ck, cv, cv, probs)


def lowered(v):
    return v.astype(BF16)


def norm_factor(v):
    return lax.rsqrt(jnp.mean(v * v, axis=-1, keepdims=True) + EPS)


def norm_back(v, gain, gy):
    r = norm_factor(v)
    part = gain * gy
    gain_part = jnp.sum(gy * v * r, axis=0)
    return r * part - v * (r * r * r) * jnp.mean(part * v, axis=-1, keepdims=True), gain_part


def position_table(length, width):
    column = jnp.arange(length + BLOCK, dtype=F32)
    distance = length - 1 - column
    rates = jnp.exp(jnp.arange(width // 2, dtype=F32) * (-2.0 * math.log(10000.0) / width))
    angles = distance[:, None] * rates[None, :]
    return jnp.concatenate([jnp.sin(angles), jnp.cos(angles)], axis=1)


SIDE = 8
CHIPS = 4
PARTS = 4
VECTORS = (0, 4, 5, 8, 13)
SINGLE = 12
SETS = ((1, 2, 3, 6), (10, 11, 7, 9), (14,), (15,))


def swap(v, bits):
    return lax.ppermute(v, "rep", [(r, r ^ bits) for r in range(SIDE)])


def shift(v, step):
    return lax.ppermute(v, "grp", [(g, (g + step) % PARTS) for g in range(PARTS)])


def total(parts):
    out = parts[0].astype(F32)
    for part in parts[1:]:
        out = out + part.astype(F32)
    return out


class Place:
    def __init__(self):
        me = lax.axis_index("rep")
        self.core = me % 2
        self.chip = me // 2
        self.grp = lax.axis_index("grp")
        self.table = jnp.stack(
            [jnp.bitwise_xor(self.chip, u) for u in range(CHIPS)]
            + [(self.grp + PARTS - s) % PARTS for s in range(PARTS)]
            + [self.core]
        ).astype(jnp.int32)


def assemble_kernel(kind, count, meta, *refs):
    locals_, mine, other, outs = refs[:count], refs[count], refs[count + 1], refs[count + 2 :]
    high = mine.shape[2]
    here = meta[CHIPS]
    core = meta[CHIPS + PARTS]
    for i in range(count):
        rows = locals_[i].shape[0]
        outs[i][pl.ds(pl.multiple_of(here * rows, 16), rows), :] = locals_[i][...]
    units = 1 if kind in ("up", "one") else CHIPS
    for u in range(units):
        src = meta[u] if units > 1 else 0
        for s in range(1, PARTS):
            k = meta[CHIPS + s]
            for ref, half in ((mine, core), (other, 1 - core)):
                row = k * 2 * high + half * high
                if kind == "down":
                    row = k * CHIPS * 2 * high + u * 2 * high + half * high
                out = outs[u] if kind == "four" else outs[0]
                out[pl.ds(pl.multiple_of(row, 16), high), :] = ref[src, s - 1]


def assemble(kind, place, locals_, mine, other):
    units, steps, high, width = mine.shape
    count = len(locals_)
    cols = width // LANES
    if kind == "up":
        grid = (CHIPS, cols)
        piece = pl.BlockSpec((1, steps, high, LANES), lambda u, j, m: (m[u], 0, 0, j))
        place_of = lambda u, j, m: (0, u * cols + j)
    else:
        grid = (cols,)
        piece = pl.BlockSpec((units, steps, high, LANES), lambda j, m: (0, 0, 0, j))
        place_of = lambda j, m: (0, j)
    shapes = [jax.ShapeDtypeStruct((PARTS * a.shape[0], a.shape[1]), a.dtype) for a in locals_]
    return pl.pallas_call(
        partial(assemble_kernel, kind, count),
        grid_spec=pltpu.PrefetchScalarGridSpec(
            num_scalar_prefetch=1,
            grid=grid,
            in_specs=[pl.BlockSpec((a.shape[0], LANES), place_of) for a in locals_] + [piece, piece],
            out_specs=[pl.BlockSpec((s.shape[0], LANES), place_of) for s in shapes],
        ),
        out_shape=shapes,
        cost_estimate=pl.CostEstimate(flops=0, transcendentals=0, bytes_accessed=sum(4 * s.shape[0] * s.shape[1] for s in shapes)),
        name="assemble_" + kind,
    )(place.table, *locals_, mine, other)


def pick(parts, index):
    out = parts[0]
    for n in range(1, len(parts)):
        out = jnp.where(index == n, parts[n], out)
    return out


def set_kind(members, local):
    if len(members) > 1:
        return "four"
    return "up" if local[members[0]].shape[1] > local[members[0]].shape[0] else "down"


def own_piece(kind, place, locals_):
    if kind == "four":
        high = locals_[0].shape[0] // 2
        return pick([lax.dynamic_slice_in_dim(a, place.core * high, high, 0) for a in locals_], place.chip)
    a = locals_[0]
    if kind == "down":
        high = a.shape[0] // SIDE
        return lax.dynamic_slice_in_dim(a, (place.chip * 2 + place.core) * high, high, 0)
    high, width = a.shape[0] // 2, a.shape[1] // CHIPS
    return lax.dynamic_slice(a, (place.core * high, place.chip * width), (high, width))


def tie(*values):
    return lax.optimization_barrier(values)


def after(values, *deps):
    out = lax.optimization_barrier((tuple(values), deps))[0]
    return list(out)


class Gather:
    def __init__(self, place, local, members):
        self.place = place
        self.members = members
        self.locals_ = [local[i] for i in members]
        self.kind = "one" if members == (SINGLE,) else set_kind(members, local)
        if self.kind == "one":
            high = self.locals_[0].shape[0] // 2
            self.own = lax.dynamic_slice_in_dim(self.locals_[0], place.core * high, high, 0)
        else:
            self.own = own_piece(self.kind, place, self.locals_)

    def along_grp(self):
        self.got = jnp.stack([shift(self.own, s) for s in range(1, PARTS)])

    def along_grp_with(self, small):
        high, width = self.own.shape
        flat = small.reshape(-1)
        extra = 8 * width - flat.shape[0]
        rows = jnp.concatenate([flat, jnp.zeros((extra,), flat.dtype)]).reshape(8, width)
        own = jnp.concatenate([self.own, rows], axis=0)
        got = [shift(own, s) for s in range(1, PARTS)]
        self.got = jnp.stack([g[:high] for g in got])
        slots = jnp.stack([small] + [g[high:].reshape(-1)[: flat.shape[0]].reshape(small.shape) for g in got])
        grp = self.place.grp
        order = [
            lax.dynamic_index_in_dim(slots, (grp + PARTS - k) % PARTS, 0, keepdims=False) for k in range(PARTS)
        ]
        return jnp.concatenate(order, axis=1)

    def in_plane(self, *deps):
        if self.kind == "one":
            self.mine = after([self.got], *deps)[0][None] if deps else self.got[None]
            return
        parts = [self.got] + [swap(self.got, 2 * b) for b in range(1, CHIPS)]
        if deps:
            parts = after(parts, *deps)
        self.mine = jnp.stack(parts)

    def between_cores(self):
        self.other = swap(self.mine, 1)

    def finish(self, full):
        for i, w in zip(self.members, assemble(self.kind, self.place, self.locals_, self.mine, self.other)):
            full[i] = w


def spread_kernel(meta, *refs):
    half = len(refs) // 2
    for n in range(half):
        refs[half + n][...] = refs[n][0, 0].astype(F32)


def spread(kind, place, stack, shapes):
    high, width = stack.shape[2:]
    block = (1, 1, high, width)
    if kind == "four":
        grid = (2,)
        ins = [pl.BlockSpec(block, lambda h, m, u=u: (m[u], jnp.bitwise_xor(h, m[CHIPS + PARTS]), 0, 0)) for u in range(CHIPS)]
        outs = [pl.BlockSpec((high, width), lambda h, m: (h, 0))] * CHIPS
    else:
        grid = (CHIPS, 2)
        ins = [pl.BlockSpec(block, lambda u, h, m: (m[u], jnp.bitwise_xor(h, m[CHIPS + PARTS]), 0, 0))]
        if kind == "down":
            outs = [pl.BlockSpec((high, width), lambda u, h, m: (2 * u + h, 0))]
        else:
            outs = [pl.BlockSpec((high, width), lambda u, h, m: (h, u))]
    return pl.pallas_call(
        spread_kernel,
        grid_spec=pltpu.PrefetchScalarGridSpec(num_scalar_prefetch=1, grid=grid, in_specs=ins, out_specs=outs),
        out_shape=[jax.ShapeDtypeStruct(s, F32) for s in shapes],
        name="spread_" + kind,
    )(place.table, *([stack] * len(ins)))


def grad_piece(kind, place, grads, unit, half):
    if kind == "four":
        a = grads[0]
        high = a.shape[3]
        out = lax.dynamic_slice(a, (unit, 0, half, 0, 0), (1, PARTS, 1, high, a.shape[4]))
        return out.reshape(PARTS, high, a.shape[4])
    rows, cols = grads[0].shape
    if kind == "down":
        high = rows // (PARTS * SIDE)
        a = grads[0].reshape(PARTS, SIDE, high, cols)
        return lax.dynamic_index_in_dim(a, 2 * unit + half, 1, keepdims=False)
    high, width = rows // (PARTS * 2), cols // CHIPS
    a = grads[0].reshape(PARTS, 2, high, cols)
    out = lax.dynamic_slice(a, (0, half, 0, unit * width), (PARTS, 1, high, width))
    return out.reshape(PARTS, high, width)


def scatter_grp(place, parts):
    send = [lax.dynamic_index_in_dim(parts, (place.grp + s) % PARTS, 0, keepdims=False) for s in range(PARTS)]
    return total([send[0]] + [shift(send[s], s) for s in range(1, PARTS)])


class Reduce:
    def __init__(self, place, kind, grads, shapes):
        self.place, self.kind, self.shapes = place, kind, shapes
        if kind == "four":
            rows, cols = grads[0].shape
            grads = [jnp.stack(grads).reshape(CHIPS, PARTS, 2, rows // (2 * PARTS), cols)]
        self.grads = grads
        self.units = [jnp.bitwise_xor(place.chip, b) for b in range(CHIPS)]
        self.send = jnp.stack([grad_piece(kind, place, grads, u, 1 - place.core) for u in self.units])

    def between_cores(self):
        got = swap(self.send, 1)
        self.sums = tuple(
            lowered(total([grad_piece(self.kind, self.place, self.grads, u, self.place.core), got[b]]))
            for b, u in enumerate(self.units)
        )

    def in_plane(self, *deps):
        parts = [self.sums[0]] + [swap(self.sums[b], 2 * b) for b in range(1, CHIPS)]
        if deps:
            parts = after(parts, *deps)
        self.part = lowered(total(parts))

    def along_grp(self):
        self.mine = lowered(scatter_grp(self.place, self.part))

    def back_plane(self):
        self.all = jnp.stack([self.mine] + [swap(self.mine, 2 * b) for b in range(1, CHIPS)])

    def finish(self):
        other = swap(self.all, 1)
        return spread(self.kind, self.place, jnp.stack([self.all, other], axis=1), self.shapes)


class ReduceSingle:
    def __init__(self, place, grad):
        rows, cols = grad.shape
        self.place = place
        self.grad = grad.reshape(PARTS, 2, rows // (2 * PARTS), cols)
        self.send = lax.dynamic_index_in_dim(self.grad, 1 - place.core, 1, keepdims=False)

    def between_cores(self):
        own = lax.dynamic_index_in_dim(self.grad, self.place.core, 1, keepdims=False)
        self.part = lowered(total([own, swap(self.send, 1)]))

    def along_grp(self):
        self.mine = lowered(scatter_grp(self.place, self.part))

    def in_plane(self):
        self.mine = lowered(total([self.mine] + [swap(self.mine, 2 * b) for b in range(1, CHIPS)]))

    def finish(self):
        other = swap(self.mine, 1)
        first = jnp.where(self.place.core == 0, self.mine, other)
        second = jnp.where(self.place.core == 0, other, self.mine)
        return jnp.concatenate([first, second], axis=0).astype(F32)


def reduce_vectors(place, small):
    for bits in (1, 2, 4):
        small = small + swap(small, bits)
    for bits in (1, 2):
        small = small + lax.ppermute(small, "grp", [(g, g ^ bits) for g in range(PARTS)])
    piece = small.shape[1] // PARTS
    return lax.dynamic_slice_in_dim(small, place.grp * piece, piece, axis=1)


def per_device(mesh_shape, tokens, docs, neighbours, neighbour_rows, out_grad, *local):
    reps, groups = mesh_shape
    fast = reps == SIDE and groups == PARTS
    rows = neighbour_rows.reshape(-1) % neighbours.shape[0]
    seqs, length, width = tokens.shape
    count = seqs * length
    near = neighbours.reshape(-1, width)
    table = lowered(position_table(length, width))
    x = tokens.reshape(count, width).astype(F32)
    full = [None] * len(local)
    place = Place()
    if fast:
        sets = [Gather(place, local, m) for m in SETS]
        single = Gather(place, local, (SINGLE,))
        vectors = sets[0].along_grp_with(jnp.stack([local[i] for i in VECTORS]))
        for n, i in enumerate(VECTORS):
            full[i] = vectors[n]
        (sets[1].own,) = after([sets[1].own], sets[0].got)
        sets[0].in_plane()
        sets[1].along_grp()
        (sets[2].own,) = after([sets[2].own], sets[1].got)
        sets[0].between_cores()
        (sets[1].got,) = after([sets[1].got], sets[0].mine)
        sets[2].along_grp()
        sets[0].finish(full)
        (sets[2].got,) = after([sets[2].got], full[1])
        single.own, sets[3].own = after([single.own, sets[3].own], sets[2].got)
        single.along_grp()
        sets[3].along_grp()
    else:
        full = [lax.all_gather(a, "grp", axis=0, tiled=True) for a in local]
    ag, bc, bp, cg, fg = (full[i].astype(F32) for i in VECTORS)
    bc, bp = bc[None], bp[None]
    normed = lowered(x * norm_factor(x) * ag)
    query = mm(normed, full[1], 1, 0)
    key = lowered(mm(normed, full[2], 1, 0))
    value = lowered(mm(normed, full[3], 1, 0))
    rel_key = lowered(mm(table, full[6], 1, 0))
    mixed, probs = self_forward(query, bc, bp, key, value, rel_key, docs)
    if fast:
        sets[1].in_plane(mixed)
        sets[2].in_plane(mixed)
        sets[1].between_cores()
        sets[3].got, single.got = after([sets[3].got, single.got], mixed)
        sets[3].in_plane()
        single.in_plane()
        single.between_cores()
        sets[2].between_cores()
        sets[1].finish(full)
    ck = lowered(mm(near, full[10], 1, 0))
    cv = lowered(mm(near, full[11], 1, 0))
    if fast:
        sets[2].other, single.other = after([sets[2].other, single.other], ck, cv)
    hidden = x + mm(mixed, full[7], 1, 0)
    cnorm = lowered(hidden * norm_factor(hidden) * cg)
    cq = lowered(mm(cnorm, full[9], 1, 0))
    if fast:
        cq, sets[3].mine = tie(cq, sets[3].mine)
        sets[3].between_cores()
    cmixed, cprobs = cross_forward(rows, cq, ck, cv, length)
    if fast:
        (sets[3].other,) = after([sets[3].other], cmixed)
        single.finish(full)
        sets[2].finish(full)
        sets[3].finish(full)
    hidden2 = hidden + mm(cmixed, full[12], 1, 0)
    fnorm = lowered(hidden2 * norm_factor(hidden2) * fg)
    upper = mm(fnorm, full[14], 1, 0)
    active = lowered(jax.nn.gelu(upper))
    result = lowered(hidden2 + mm(active, full[15], 1, 0))

    gy = out_grad.reshape(count, width)
    g_down = lowered(mm(active, gy, 0, 0))
    if fast:
        r_down = Reduce(place, "down", [g_down], [local[15].shape])
        gy, r_down.send, result = tie(gy, r_down.send, result)
    g_active = mm(gy, full[15], 1, 1)
    g_upper = lowered(jax.vjp(jax.nn.gelu, upper)[1](g_active)[0])
    g_up = lowered(mm(fnorm, g_upper, 0, 0))
    if fast:
        r_down.between_cores()
        r_up = Reduce(place, "up", [g_up], [local[14].shape])
        g_upper, r_up.send, r_down.sums = tie(g_upper, r_up.send, r_down.sums)
        r_down.in_plane()
    g_fnorm = mm(g_upper, full[14], 1, 1)
    part, g_fg = norm_back(hidden2, fg, g_fnorm)
    g_h2 = gy.astype(F32) + part
    g_branch = lowered(g_h2)
    g_cproj = lowered(mm(cmixed, g_branch, 0, 0))
    g_cmixed = lowered(mm(g_branch, full[12], 1, 1))
    if fast:
        r_up.between_cores()
        r_one = ReduceSingle(place, g_cproj)
        g_cmixed, r_up.sums, r_one.send = tie(g_cmixed, r_up.sums, r_one.send)
        r_one.between_cores()
        r_up.in_plane()
    g_cq, g_ck, g_cv = cross_backward(rows, cq, g_cmixed, ck, cv, cprobs, length)
    if fast:
        g_cq, r_down.part, r_up.part, r_one.part = tie(g_cq, r_down.part, r_up.part, r_one.part)
        r_one.along_grp()
        r_down.along_grp()
        r_up.along_grp()
    g_cquery_w = lowered(mm(cnorm, g_cq, 0, 0))
    g_ckey_w = lowered(mm(near, g_ck, 0, 0))
    g_cvalue_w = lowered(mm(near, g_cv, 0, 0))
    g_cnorm = mm(g_cq, full[9], 1, 1)
    part, g_cg = norm_back(hidden, cg, g_cnorm)
    g_h1 = g_h2 + part
    g_attn = lowered(g_h1)
    g_aproj = lowered(mm(mixed, g_attn, 0, 0))
    if fast:
        r_cross = Reduce(place, "four", [g_ckey_w, g_cvalue_w, g_aproj, g_cquery_w], [local[10].shape] * CHIPS)
        g_attn, r_cross.send = tie(g_attn, r_cross.send)
    g_near = lowered(mm(g_ck, full[10], 1, 1) + mm(g_cv, full[11], 1, 1)).reshape(neighbours.shape)
    g_mixed = lowered(mm(g_attn, full[7], 1, 1))
    if fast:
        r_cross.between_cores()
        g_mixed, g_near, r_cross.sums, r_one.mine = tie(g_mixed, g_near, r_cross.sums, r_one.mine)
        r_cross.in_plane()
        r_one.in_plane()
    g_q, g_k, g_v, g_relk, g_bc, g_bp = self_backward(query, bc, bp, key, value, rel_key, g_mixed, probs)
    if fast:
        g_q, g_k, g_v, r_down.mine, r_up.mine, r_one.mine, r_cross.part = tie(
            g_q, g_k, g_v, r_down.mine, r_up.mine, r_one.mine, r_cross.part
        )
        r_down.back_plane()
        r_up.back_plane()
        r_cross.along_grp()
    g_rel_sum = lowered(jnp.sum(g_relk.astype(F32), axis=0))
    g_rel = lowered(mm(table, g_rel_sum, 0, 0))
    g_query_w = lowered(mm(normed, g_q, 0, 0))
    g_key_w = lowered(mm(normed, g_k, 0, 0))
    g_value_w = lowered(mm(normed, g_v, 0, 0))
    if fast:
        r_self = Reduce(place, "four", [g_query_w, g_key_w, g_value_w, g_rel], [local[1].shape] * CHIPS)
        g_q, g_k, g_v, r_self.send = tie(g_q, g_k, g_v, r_self.send)
        r_self.between_cores()
    g_normed = mm(g_q, full[1], 1, 1) + mm(g_k, full[2], 1, 1) + mm(g_v, full[3], 1, 1)
    part, g_ag = norm_back(x, ag, g_normed)
    grad_x = lowered(g_h1 + part)
    small = [g_ag, g_bc[0], g_bp[0], g_cg, g_fg]
    out = [None] * len(local)
    if fast:
        r_cross.back_plane()
        out[SINGLE] = r_one.finish()
        out[15] = r_down.finish()[0]
        out[14] = r_up.finish()[0]
        r_self.in_plane(out[14], out[15], grad_x)
        r_self.along_grp()
        r_self.back_plane()
        vectors = reduce_vectors(place, jnp.stack(small))
        for n, i in enumerate(VECTORS):
            out[i] = vectors[n]
        for i, w in zip((10, 11, 7, 9), r_cross.finish()):
            out[i] = w
        for i, w in zip((1, 2, 3, 6), r_self.finish()):
            out[i] = w
    else:
        grads = [None, g_query_w, g_key_w, g_value_w, None, None, g_rel, g_aproj, None, g_cquery_w, g_ckey_w,
                 g_cvalue_w, g_cproj, None, g_up, g_down]
        for n, i in enumerate(VECTORS):
            grads[i] = small[n]
        for i, g in enumerate(grads):
            shard = lax.psum_scatter(lowered(g), "grp", scatter_dimension=0, tiled=True)
            out[i] = lax.psum(shard.astype(F32), "rep")
    return (result.reshape(tokens.shape), grad_x.reshape(tokens.shape), g_near) + tuple(out)


def solution(mesh):
    data3 = P(("rep", "grp"), None, None)
    data2 = P(("rep", "grp"), None)
    ranks = (1, 2, 2, 2, 1, 1, 2, 2, 1, 2, 2, 2, 2, 1, 2, 2)
    weights = tuple(P("grp") if r == 1 else P("grp", None) for r in ranks)
    return jax.shard_map(
        partial(per_device, (mesh.shape["rep"], mesh.shape["grp"])),
        mesh=mesh,
        in_specs=(data3, data2, data3, data2, data3) + weights,
        out_specs=(data3, data3, data3) + weights,
        check_vma=False,
    )
```

```python
import math
from functools import partial
import jax
import jax.numpy as jnp
from jax import lax
from jax.sharding import PartitionSpec as P
from jax.experimental import pallas as pl
from jax.experimental.pallas import tpu as pltpu

HEADS = 14
HDIM = 64
STRETCH = 64
NEIGH = 2
NLEN = 128
BLOCK = 256
LANES = 128
EPS = 1e-06
NEG = -1000000000.0
SCALE = HDIM ** -0.5
F32 = jnp.float32
BF16 = jnp.bfloat16


def busy(us):
    return pl.CostEstimate(flops=int(us * 1e9), transcendentals=0, bytes_accessed=int(us * 3e6))


def mm(a, b, ca, cb):
    return lax.dot_general(a, b, (((ca,), (cb,)), ((), ())), preferred_element_type=F32)


def low_lanes(shape):
    return lax.broadcasted_iota(jnp.int32, shape, len(shape) - 1) < HDIM


def self_fwd_kernel(q_ref, bc_ref, bp_ref, k_ref, v_ref, rel_ref, dr_ref, dc_ref, mixed_ref, *p_refs):
    length = k_ref.shape[0]
    query = q_ref[...]
    content_q = (query + bc_ref[...]).astype(BF16)
    position_q = (query + bp_ref[...]).astype(BF16)
    lo = low_lanes((1, LANES))
    masks = (lo, jnp.logical_not(lo))
    for index in range(length // BLOCK):
        first = index * BLOCK
        keys = first + BLOCK
        span = keys + BLOCK
        rel = rel_ref[length - keys : length - keys + span, :]
        cq = content_q[first:keys] * BF16(SCALE)
        pq = position_q[first:keys] * BF16(SCALE)
        same = dc_ref[0, first:keys, :] == dr_ref[0, :, :keys]
        outs = []
        for head in range(2):
            zero = jnp.zeros((), BF16)
            content = mm(jnp.where(masks[head], cq, zero), k_ref[:keys, :], 1, 1)
            full = mm(jnp.where(masks[head], pq, zero), rel, 1, 1)
            moved = pltpu.roll(full, span - BLOCK + 1, 1, stride=1, stride_axis=0)
            s = jnp.where(same, content + moved[:, :keys], NEG)
            e = jnp.exp(s - jnp.max(s, axis=1, keepdims=True))
            p = (e * (1.0 / jnp.sum(e, axis=1, keepdims=True))).astype(BF16)
            p_refs[index][0, 0, head] = p
            outs.append(mm(p, v_ref[:keys, :], 1, 0))
        mixed_ref[first:keys, :] = jnp.where(lo, outs[0], outs[1]).astype(BF16)


def self_bwd_kernel(q_ref, bc_ref, bp_ref, k_ref, v_ref, rel_ref, gm_ref, *refs):
    nblk = k_ref.shape[0] // BLOCK
    p_refs = refs[:nblk]
    gq_ref, gk_ref, gv_ref, grel_ref, gbc_ref, gbp_ref = refs[nblk : nblk + 6]
    gvt, gkt, grelt = refs[nblk + 6 :]
    length = k_ref.shape[0]
    seq = pl.program_id(1)
    query = q_ref[...]
    content_q = (query + bc_ref[...]).astype(BF16)
    position_q = (query + bp_ref[...]).astype(BF16)
    flip = (
        lax.broadcasted_iota(jnp.int32, (BLOCK, BLOCK), 0) + lax.broadcasted_iota(jnp.int32, (BLOCK, BLOCK), 1)
        == BLOCK - 1
    ).astype(BF16)
    gm = gm_ref[...]
    gmt = jnp.transpose(gm.astype(F32)).astype(BF16)
    lo = low_lanes((1, LANES))
    masks = (lo, jnp.logical_not(lo))
    zero = jnp.zeros((), BF16)
    gvt[...] = jnp.zeros_like(gvt)
    gkt[...] = jnp.zeros_like(gkt)
    grelt[...] = jnp.zeros_like(grelt)
    sum_c = jnp.zeros((1, LANES), F32)
    sum_p = jnp.zeros((1, LANES), F32)
    for index in range(nblk):
        first = index * BLOCK
        keys = first + BLOCK
        span = keys + BLOCK
        start = length - keys
        rel = rel_ref[start : start + span, :]
        gm_r = mm(flip, gm[first:keys], 1, 0).astype(BF16)
        cqt = jnp.transpose(mm(flip, content_q[first:keys] * BF16(SCALE), 1, 0)).astype(BF16)
        pqt = jnp.transpose(mm(flip, position_q[first:keys] * BF16(SCALE), 1, 0)).astype(BF16)
        gcs = []
        gps = []
        for head in range(2):
            hs = slice(head * HDIM, (head + 1) * HDIM)
            p = p_refs[index][0, 0, head]
            pf = mm(flip, p, 1, 0)
            g_p = mm(jnp.where(masks[head], gm_r, zero), v_ref[:keys, :], 1, 1)
            delta = jnp.sum(pf * g_p, axis=1, keepdims=True)
            gsf = pf * (g_p - delta)
            gs = gsf.astype(BF16)
            gvt[hs, :keys] += mm(gmt[hs, first:keys], p, 1, 0)
            gkt[hs, :keys] += mm(cqt[hs], gs, 1, 0)
            gcs.append(mm(gs, k_ref[:keys, :], 1, 0))
            padded = jnp.concatenate([gsf, jnp.zeros((BLOCK, BLOCK), F32)], axis=1)
            grel = pltpu.roll(padded, 0, 1, stride=1, stride_axis=0).astype(BF16)
            gps.append(mm(grel, rel, 1, 0))
            grelt[hs, start : start + span] += mm(pqt[hs], grel, 1, 0)
        gc = jnp.where(lo, gcs[0], gcs[1]) * SCALE
        gp = jnp.where(lo, gps[0], gps[1]) * SCALE
        sum_c += jnp.sum(gc, axis=0, keepdims=True)
        sum_p += jnp.sum(gp, axis=0, keepdims=True)
        gq_ref[first:keys, :] = mm(flip, (gc + gp).astype(BF16), 1, 0).astype(BF16)
    gv_ref[...] = jnp.transpose(gvt[...]).astype(BF16)
    gk_ref[...] = jnp.transpose(gkt[...]).astype(BF16)
    grel_ref[0] = jnp.transpose(grelt[...]).astype(BF16)

    @pl.when(seq == 0)
    def _():
        gbc_ref[...] = sum_c
        gbp_ref[...] = sum_p

    @pl.when(seq > 0)
    def _():
        gbc_ref[...] += sum_c
        gbp_ref[...] += sum_p


def self_specs(seqs, length, width):
    pairs = width // LANES
    table = length + BLOCK
    tok = pl.BlockSpec((length, LANES), lambda h, s: (s, h))
    vec = pl.BlockSpec((1, LANES), lambda h, s: (0, h))
    rel = pl.BlockSpec((table, LANES), lambda h, s: (0, h))
    probs = [
        pl.BlockSpec((1, 1, 2, BLOCK, (i + 1) * BLOCK), lambda h, s: (h, s, 0, 0, 0))
        for i in range(length // BLOCK)
    ]
    shapes = [
        jax.ShapeDtypeStruct((pairs, seqs, 2, BLOCK, (i + 1) * BLOCK), BF16)
        for i in range(length // BLOCK)
    ]
    return (pairs, seqs), tok, vec, rel, probs, shapes


def self_forward(query, bc, bp, key, value, rel_key, docs):
    seqs, length = docs.shape
    width = query.shape[1]
    grid, tok, vec, rel, pspecs, pshapes = self_specs(seqs, length, width)
    outs = pl.pallas_call(
        self_fwd_kernel,
        grid=grid,
        in_specs=[
            tok, vec, vec, tok, tok, rel,
            pl.BlockSpec((1, 1, length), lambda h, s: (s, 0, 0)),
            pl.BlockSpec((1, length, 1), lambda h, s: (s, 0, 0)),
        ],
        out_specs=[tok] + pspecs,
        out_shape=[jax.ShapeDtypeStruct(query.shape, BF16)] + pshapes,
        cost_estimate=busy(41),
        name="self_fwd",
    )(query, bc, bp, key, value, rel_key, docs[:, None, :], docs[:, :, None])
    return outs[0], outs[1:]


def self_backward(query, bc, bp, key, value, rel_key, g_mixed, probs):
    width = query.shape[1]
    seqs = probs[0].shape[1]
    length = query.shape[0] // seqs
    grid, tok, vec, rel, pspecs, _ = self_specs(seqs, length, width)
    table = length + BLOCK
    tshape = jax.ShapeDtypeStruct(query.shape, BF16)
    vshape = jax.ShapeDtypeStruct((1, width), F32)
    return pl.pallas_call(
        self_bwd_kernel,
        grid=grid,
        in_specs=[tok, vec, vec, tok, tok, rel, tok] + pspecs,
        out_specs=[tok, tok, tok, pl.BlockSpec((1, table, LANES), lambda h, s: (s, 0, h)), vec, vec],
        out_shape=[tshape, tshape, tshape, jax.ShapeDtypeStruct((seqs, table, width), BF16), vshape, vshape],
        scratch_shapes=[
            pltpu.VMEM((LANES, length), F32),
            pltpu.VMEM((LANES, length), F32),
            pltpu.VMEM((LANES, table), F32),
        ],
        cost_estimate=busy(43),
        name="self_bwd",
    )(query, bc, bp, key, value, rel_key, g_mixed, *probs)


def shift_up(v):
    return pltpu.roll(v, v.shape[0] - STRETCH + 1, 0)


def shift_down(v):
    moved = pltpu.roll(v, STRETCH - 1, 0)
    row = lax.broadcasted_iota(jnp.int32, (v.shape[0], 1), 0)
    return jnp.where(row >= STRETCH - 1, moved, 0.0)


def both_heads(v, lo):
    zero = jnp.zeros((), BF16)
    return jnp.concatenate([jnp.where(lo, v, zero), jnp.where(lo, zero, v)], axis=0)


def cross_fwd_kernel(rows_ref, q_ref, k0_ref, k1_ref, v0_ref, v1_ref, out_ref, p_ref, qs, os):
    u = pl.program_id(1)
    lo = low_lanes((1, LANES))

    @pl.when(u == 0)
    def _():
        qs[...] = shift_up(q_ref[...].astype(F32) * SCALE).astype(BF16)

    place = pl.ds(pl.multiple_of(u * STRETCH, STRETCH), STRETCH)
    for pair in range(q_ref.shape[1] // LANES):
        cols = slice(pair * LANES, (pair + 1) * LANES)
        q = both_heads(qs[place, cols], lo)
        k = jnp.concatenate([k0_ref[:, cols], k1_ref[:, cols]], axis=0)
        v = jnp.concatenate([v0_ref[:, cols], v1_ref[:, cols]], axis=0)
        s = mm(q, k, 1, 1)
        e = jnp.exp(s - jnp.max(s, axis=1, keepdims=True))
        p = (e * (1.0 / jnp.sum(e, axis=1, keepdims=True))).astype(BF16)
        p_ref[0, pair] = p
        o = mm(p, v, 1, 0)
        os[place, cols] = jnp.where(lo, o[:STRETCH], o[STRETCH:])

    @pl.when(u == pl.num_programs(1) - 1)
    def _():
        out_ref[...] = shift_down(os[...]).astype(BF16)


def cross_bwd_kernel(rows_ref, q_ref, g_ref, k0_ref, k1_ref, v0_ref, v1_ref, p_ref,
                     gq_ref, gk_ref, gv_ref, qs, gs_s, gq_s, gk_s, gv_s):
    u = pl.program_id(1)
    n = pl.program_id(2)
    lo = low_lanes((1, LANES))

    @pl.when(jnp.logical_and(u == 0, n == 0))
    def _():
        qs[...] = shift_up(q_ref[...].astype(F32) * SCALE).astype(BF16)
        g = g_ref[...].astype(F32)
        row = lax.broadcasted_iota(jnp.int32, (g.shape[0], 1), 0)
        gs_s[...] = shift_up(jnp.where(row >= STRETCH - 1, g, 0.0)).astype(BF16)

    @pl.when(n == 0)
    def _():
        place = pl.ds(pl.multiple_of(u * STRETCH, STRETCH), STRETCH)
        for pair in range(q_ref.shape[1] // LANES):
            cols = slice(pair * LANES, (pair + 1) * LANES)
            q = both_heads(qs[place, cols], lo)
            g = both_heads(gs_s[place, cols], lo)
            k = jnp.concatenate([k0_ref[:, cols], k1_ref[:, cols]], axis=0)
            v = jnp.concatenate([v0_ref[:, cols], v1_ref[:, cols]], axis=0)
            p = p_ref[0, pair]
            pf = p.astype(F32)
            g_p = mm(g, v, 1, 1)
            delta = jnp.sum(pf * g_p, axis=1, keepdims=True)
            gs = (pf * (g_p - delta)).astype(BF16)
            gv = mm(p, g, 0, 0).astype(BF16)
            gk = mm(gs, q, 0, 0).astype(BF16)
            gq = mm(gs, k, 1, 0)
            gq_s[place, cols] = jnp.where(lo, gq[:STRETCH], gq[STRETCH:]) * SCALE
            gk_ref[:, cols] = gk[:NLEN]
            gv_ref[:, cols] = gv[:NLEN]
            gk_s[:, cols] = gk[NLEN:]
            gv_s[:, cols] = gv[NLEN:]

    @pl.when(n == 1)
    def _():
        gk_ref[...] = gk_s[...]
        gv_ref[...] = gv_s[...]

    @pl.when(jnp.logical_and(u == pl.num_programs(1) - 1, n == 1))
    def _():
        gq_ref[...] = shift_down(gq_s[...]).astype(BF16)


def cross_forward(rows, cq, ck, cv, length):
    tokens, width = cq.shape
    seqs = tokens // length
    per = length // STRETCH
    pairs = width // LANES
    tok = pl.BlockSpec((length, width), lambda s, u, r: (s, 0))
    near = [
        pl.BlockSpec((NLEN, width), lambda s, u, r, n=n: (r[(s * per + u) * NEIGH + n], 0))
        for n in range(NEIGH)
    ]
    return pl.pallas_call(
        cross_fwd_kernel,
        grid_spec=pltpu.PrefetchScalarGridSpec(
            num_scalar_prefetch=1,
            grid=(seqs, per),
            in_specs=[tok] + near + near,
            out_specs=[
                tok,
                pl.BlockSpec((1, pairs, 2 * STRETCH, NEIGH * NLEN), lambda s, u, r: (s * per + u, 0, 0, 0)),
            ],
            scratch_shapes=[pltpu.VMEM((length, width), BF16), pltpu.VMEM((length, width), F32)],
        ),
        out_shape=[
            jax.ShapeDtypeStruct(cq.shape, BF16),
            jax.ShapeDtypeStruct((seqs * per, pairs, 2 * STRETCH, NEIGH * NLEN), BF16),
        ],
        cost_estimate=busy(24),
        name="cross_fwd",
    )(rows, cq, ck, ck, cv, cv)


def cross_backward(rows, cq, g_cmixed, ck, cv, probs, length):
    tokens, width = cq.shape
    seqs = tokens // length
    per = length // STRETCH
    pairs = width // LANES
    tok = pl.BlockSpec((length, width), lambda s, u, n, r: (s, 0))
    near = [
        pl.BlockSpec((NLEN, width), lambda s, u, n, r, m=m: (r[(s * per + u) * NEIGH + m], 0))
        for m in range(NEIGH)
    ]
    out = pl.BlockSpec((NLEN, width), lambda s, u, n, r: (r[(s * per + u) * NEIGH + n], 0))
    return pl.pallas_call(
        cross_bwd_kernel,
        grid_spec=pltpu.PrefetchScalarGridSpec(
            num_scalar_prefetch=1,
            grid=(seqs, per, NEIGH),
            in_specs=[tok, tok] + near + near + [
                pl.BlockSpec((1, pairs, 2 * STRETCH, NEIGH * NLEN), lambda s, u, n, r: (s * per + u, 0, 0, 0)),
            ],
            out_specs=[tok, out, out],
            scratch_shapes=[
                pltpu.VMEM((length, width), BF16),
                pltpu.VMEM((length, width), BF16),
                pltpu.VMEM((length, width), F32),
                pltpu.VMEM((NLEN, width), BF16),
                pltpu.VMEM((NLEN, width), BF16),
            ],
        ),
        out_shape=[
            jax.ShapeDtypeStruct(cq.shape, BF16),
            jax.ShapeDtypeStruct(ck.shape, BF16),
            jax.ShapeDtypeStruct(cv.shape, BF16),
        ],
        cost_estimate=busy(70),
        name="cross_bwd",
    )(rows, cq, g_cmixed, ck, ck, cv, cv, probs)


def lowered(v):
    return v.astype(BF16)


def norm_factor(v):
    return lax.rsqrt(jnp.mean(v * v, axis=-1, keepdims=True) + EPS)


def norm_back(v, gain, gy):
    r = norm_factor(v)
    part = gain * gy
    gain_part = jnp.sum(gy * v * r, axis=0)
    return r * part - v * (r * r * r) * jnp.mean(part * v, axis=-1, keepdims=True), gain_part


def position_table(length, width):
    column = jnp.arange(length + BLOCK, dtype=F32)
    distance = length - 1 - column
    rates = jnp.exp(jnp.arange(width // 2, dtype=F32) * (-2.0 * math.log(10000.0) / width))
    angles = distance[:, None] * rates[None, :]
    return jnp.concatenate([jnp.sin(angles), jnp.cos(angles)], axis=1)


SIDE = 8
CHIPS = 4
PARTS = 4
VECTORS = (0, 4, 5, 8, 13)
SINGLE = 12
SETS = ((1, 2, 3, 6), (10, 11, 7, 9), (14,), (15,))


def swap(v, bits):
    return lax.ppermute(v, "rep", [(r, r ^ bits) for r in range(SIDE)])


def shift(v, step):
    return lax.ppermute(v, "grp", [(g, (g + step) % PARTS) for g in range(PARTS)])


def total(parts):
    out = parts[0].astype(F32)
    for part in parts[1:]:
        out = out + part.astype(F32)
    return out


class Place:
    def __init__(self):
        me = lax.axis_index("rep")
        self.core = me % 2
        self.chip = me // 2
        self.grp = lax.axis_index("grp")
        self.table = jnp.stack(
            [jnp.bitwise_xor(self.chip, u) for u in range(CHIPS)]
            + [(self.grp + PARTS - s) % PARTS for s in range(PARTS)]
            + [self.core]
        ).astype(jnp.int32)


def assemble_kernel(kind, count, meta, *refs):
    locals_, mine, other, outs = refs[:count], refs[count], refs[count + 1], refs[count + 2 :]
    high = mine.shape[2]
    here = meta[CHIPS]
    core = meta[CHIPS + PARTS]
    for i in range(count):
        rows = locals_[i].shape[0]
        outs[i][pl.ds(pl.multiple_of(here * rows, 16), rows), :] = locals_[i][...]
    units = 1 if kind in ("up", "one") else CHIPS
    for u in range(units):
        src = meta[u] if units > 1 else 0
        for s in range(1, PARTS):
            k = meta[CHIPS + s]
            for ref, half in ((mine, core), (other, 1 - core)):
                row = k * 2 * high + half * high
                if kind == "down":
                    row = k * CHIPS * 2 * high + u * 2 * high + half * high
                out = outs[u] if kind == "four" else outs[0]
                out[pl.ds(pl.multiple_of(row, 16), high), :] = ref[src, s - 1]


def assemble(kind, place, locals_, mine, other):
    units, steps, high, width = mine.shape
    count = len(locals_)
    cols = width // LANES
    if kind == "up":
        grid = (CHIPS, cols)
        piece = pl.BlockSpec((1, steps, high, LANES), lambda u, j, m: (m[u], 0, 0, j))
        place_of = lambda u, j, m: (0, u * cols + j)
    else:
        grid = (cols,)
        piece = pl.BlockSpec((units, steps, high, LANES), lambda j, m: (0, 0, 0, j))
        place_of = lambda j, m: (0, j)
    shapes = [jax.ShapeDtypeStruct((PARTS * a.shape[0], a.shape[1]), a.dtype) for a in locals_]
    return pl.pallas_call(
        partial(assemble_kernel, kind, count),
        grid_spec=pltpu.PrefetchScalarGridSpec(
            num_scalar_prefetch=1,
            grid=grid,
            in_specs=[pl.BlockSpec((a.shape[0], LANES), place_of) for a in locals_] + [piece, piece],
            out_specs=[pl.BlockSpec((s.shape[0], LANES), place_of) for s in shapes],
        ),
        out_shape=shapes,
        cost_estimate=busy(9),
        name="assemble_" + kind,
    )(place.table, *locals_, mine, other)


def pick(parts, index):
    out = parts[0]
    for n in range(1, len(parts)):
        out = jnp.where(index == n, parts[n], out)
    return out


def set_kind(members, local):
    if len(members) > 1:
        return "four"
    return "up" if local[members[0]].shape[1] > local[members[0]].shape[0] else "down"


def own_piece(kind, place, locals_):
    if kind == "four":
        high = locals_[0].shape[0] // 2
        return pick([lax.dynamic_slice_in_dim(a, place.core * high, high, 0) for a in locals_], place.chip)
    a = locals_[0]
    if kind == "down":
        high = a.shape[0] // SIDE
        return lax.dynamic_slice_in_dim(a, (place.chip * 2 + place.core) * high, high, 0)
    high, width = a.shape[0] // 2, a.shape[1] // CHIPS
    return lax.dynamic_slice(a, (place.core * high, place.chip * width), (high, width))


def tie(*values):
    return lax.optimization_barrier(values)


def after(values, *deps):
    out = lax.optimization_barrier((tuple(values), deps))[0]
    return list(out)


class Gather:
    def __init__(self, place, local, members):
        self.place = place
        self.members = members
        self.locals_ = [local[i] for i in members]
        self.kind = "one" if members == (SINGLE,) else set_kind(members, local)
        if self.kind == "one":
            high = self.locals_[0].shape[0] // 2
            self.own = lax.dynamic_slice_in_dim(self.locals_[0], place.core * high, high, 0)
        else:
            self.own = own_piece(self.kind, place, self.locals_)

    def along_grp(self):
        self.got = jnp.stack([shift(self.own, s) for s in range(1, PARTS)])

    def along_grp_with(self, small):
        high, width = self.own.shape
        flat = small.reshape(-1)
        extra = 8 * width - flat.shape[0]
        rows = jnp.concatenate([flat, jnp.zeros((extra,), flat.dtype)]).reshape(8, width)
        own = jnp.concatenate([self.own, rows], axis=0)
        got = [shift(own, s) for s in range(1, PARTS)]
        self.got = jnp.stack([g[:high] for g in got])
        slots = jnp.stack([small] + [g[high:].reshape(-1)[: flat.shape[0]].reshape(small.shape) for g in got])
        grp = self.place.grp
        order = [
            lax.dynamic_index_in_dim(slots, (grp + PARTS - k) % PARTS, 0, keepdims=False) for k in range(PARTS)
        ]
        return jnp.concatenate(order, axis=1)

    def in_plane(self, *deps):
        if self.kind == "one":
            self.mine = after([self.got], *deps)[0][None] if deps else self.got[None]
            return
        parts = [self.got] + [swap(self.got, 2 * b) for b in range(1, CHIPS)]
        if deps:
            parts = after(parts, *deps)
        self.mine = jnp.stack(parts)

    def between_cores(self):
        self.other = swap(self.mine, 1)

    def finish(self, full):
        for i, w in zip(self.members, assemble(self.kind, self.place, self.locals_, self.mine, self.other)):
            full[i] = w


def spread_kernel(meta, *refs):
    half = len(refs) // 2
    for n in range(half):
        refs[half + n][...] = refs[n][0, 0].astype(F32)


def spread(kind, place, stack, shapes):
    high, width = stack.shape[2:]
    block = (1, 1, high, width)
    if kind == "four":
        grid = (2,)
        ins = [pl.BlockSpec(block, lambda h, m, u=u: (m[u], jnp.bitwise_xor(h, m[CHIPS + PARTS]), 0, 0)) for u in range(CHIPS)]
        outs = [pl.BlockSpec((high, width), lambda h, m: (h, 0))] * CHIPS
    else:
        grid = (CHIPS, 2)
        ins = [pl.BlockSpec(block, lambda u, h, m: (m[u], jnp.bitwise_xor(h, m[CHIPS + PARTS]), 0, 0))]
        if kind == "down":
            outs = [pl.BlockSpec((high, width), lambda u, h, m: (2 * u + h, 0))]
        else:
            outs = [pl.BlockSpec((high, width), lambda u, h, m: (h, u))]
    return pl.pallas_call(
        spread_kernel,
        grid_spec=pltpu.PrefetchScalarGridSpec(num_scalar_prefetch=1, grid=grid, in_specs=ins, out_specs=outs),
        out_shape=[jax.ShapeDtypeStruct(s, F32) for s in shapes],
        cost_estimate=busy(5),
        name="spread_" + kind,
    )(place.table, *([stack] * len(ins)))


def grad_piece(kind, place, grads, unit, half):
    if kind == "four":
        a = grads[0]
        high = a.shape[3]
        out = lax.dynamic_slice(a, (unit, 0, half, 0, 0), (1, PARTS, 1, high, a.shape[4]))
        return out.reshape(PARTS, high, a.shape[4])
    rows, cols = grads[0].shape
    if kind == "down":
        high = rows // (PARTS * SIDE)
        a = grads[0].reshape(PARTS, SIDE, high, cols)
        return lax.dynamic_index_in_dim(a, 2 * unit + half, 1, keepdims=False)
    high, width = rows // (PARTS * 2), cols // CHIPS
    a = grads[0].reshape(PARTS, 2, high, cols)
    out = lax.dynamic_slice(a, (0, half, 0, unit * width), (PARTS, 1, high, width))
    return out.reshape(PARTS, high, width)


def scatter_grp(place, parts):
    send = [lax.dynamic_index_in_dim(parts, (place.grp + s) % PARTS, 0, keepdims=False) for s in range(PARTS)]
    return total([send[0]] + [shift(send[s], s) for s in range(1, PARTS)])


class Reduce:
    def __init__(self, place, kind, grads, shapes):
        self.place, self.kind, self.shapes = place, kind, shapes
        if kind == "four":
            rows, cols = grads[0].shape
            grads = [jnp.stack(grads).reshape(CHIPS, PARTS, 2, rows // (2 * PARTS), cols)]
        self.grads = grads
        self.units = [jnp.bitwise_xor(place.chip, b) for b in range(CHIPS)]
        self.send = jnp.stack([grad_piece(kind, place, grads, u, 1 - place.core) for u in self.units])

    def between_cores(self):
        got = swap(self.send, 1)
        self.sums = tuple(
            lowered(total([grad_piece(self.kind, self.place, self.grads, u, self.place.core), got[b]]))
            for b, u in enumerate(self.units)
        )

    def in_plane(self, *deps):
        parts = [self.sums[0]] + [swap(self.sums[b], 2 * b) for b in range(1, CHIPS)]
        if deps:
            parts = after(parts, *deps)
        self.part = lowered(total(parts))

    def along_grp(self):
        self.mine = lowered(scatter_grp(self.place, self.part))

    def back_plane(self):
        self.all = jnp.stack([self.mine] + [swap(self.mine, 2 * b) for b in range(1, CHIPS)])

    def finish(self):
        other = swap(self.all, 1)
        return spread(self.kind, self.place, jnp.stack([self.all, other], axis=1), self.shapes)


class ReduceSingle:
    def __init__(self, place, grad):
        rows, cols = grad.shape
        self.place = place
        self.grad = grad.reshape(PARTS, 2, rows // (2 * PARTS), cols)
        self.send = lax.dynamic_index_in_dim(self.grad, 1 - place.core, 1, keepdims=False)

    def between_cores(self):
        own = lax.dynamic_index_in_dim(self.grad, self.place.core, 1, keepdims=False)
        self.part = lowered(total([own, swap(self.send, 1)]))

    def along_grp(self):
        self.mine = lowered(scatter_grp(self.place, self.part))

    def in_plane(self):
        self.mine = lowered(total([self.mine] + [swap(self.mine, 2 * b) for b in range(1, CHIPS)]))

    def finish(self):
        other = swap(self.mine, 1)
        first = jnp.where(self.place.core == 0, self.mine, other)
        second = jnp.where(self.place.core == 0, other, self.mine)
        return jnp.concatenate([first, second], axis=0).astype(F32)


def reduce_vectors(place, small):
    for bits in (1, 2, 4):
        small = small + swap(small, bits)
    for bits in (1, 2):
        small = small + lax.ppermute(small, "grp", [(g, g ^ bits) for g in range(PARTS)])
    piece = small.shape[1] // PARTS
    return lax.dynamic_slice_in_dim(small, place.grp * piece, piece, axis=1)


def per_device(mesh_shape, tokens, docs, neighbours, neighbour_rows, out_grad, *local):
    reps, groups = mesh_shape
    fast = reps == SIDE and groups == PARTS
    rows = neighbour_rows.reshape(-1) % neighbours.shape[0]
    seqs, length, width = tokens.shape
    count = seqs * length
    near = neighbours.reshape(-1, width)
    table = lowered(position_table(length, width))
    x = tokens.reshape(count, width).astype(F32)
    full = [None] * len(local)
    place = Place()
    if fast:
        sets = [Gather(place, local, m) for m in SETS]
        single = Gather(place, local, (SINGLE,))
        vectors = sets[0].along_grp_with(jnp.stack([local[i] for i in VECTORS]))
        for n, i in enumerate(VECTORS):
            full[i] = vectors[n]
        (sets[1].own,) = after([sets[1].own], sets[0].got)
        sets[0].in_plane()
        sets[1].along_grp()
        (sets[2].own,) = after([sets[2].own], sets[1].got)
        sets[0].between_cores()
        (sets[1].got,) = after([sets[1].got], sets[0].mine)
        sets[2].along_grp()
        sets[0].finish(full)
        (sets[2].got,) = after([sets[2].got], full[1])
        single.own, sets[3].own = after([single.own, sets[3].own], sets[2].got)
        single.along_grp()
        sets[3].along_grp()
    else:
        full = [lax.all_gather(a, "grp", axis=0, tiled=True) for a in local]
    ag, bc, bp, cg, fg = (full[i].astype(F32) for i in VECTORS)
    bc, bp = bc[None], bp[None]
    normed = lowered(x * norm_factor(x) * ag)
    query = mm(normed, full[1], 1, 0)
    key = lowered(mm(normed, full[2], 1, 0))
    value = lowered(mm(normed, full[3], 1, 0))
    rel_key = lowered(mm(table, full[6], 1, 0))
    mixed, probs = self_forward(query, bc, bp, key, value, rel_key, docs)
    if fast:
        sets[1].in_plane()
        sets[2].in_plane()
        mixed, sets[1].mine, sets[2].mine, sets[3].got, single.got = tie(
            mixed, sets[1].mine, sets[2].mine, sets[3].got, single.got
        )
        sets[1].between_cores()
        sets[3].in_plane()
        single.in_plane()
        single.between_cores()
        sets[2].between_cores()
        sets[1].finish(full)
    ck = lowered(mm(near, full[10], 1, 0))
    cv = lowered(mm(near, full[11], 1, 0))
    if fast:
        ck, cv, sets[2].other, single.other, mixed = tie(ck, cv, sets[2].other, single.other, mixed)
    hidden = x + mm(mixed, full[7], 1, 0)
    cnorm = lowered(hidden * norm_factor(hidden) * cg)
    cq = lowered(mm(cnorm, full[9], 1, 0))
    if fast:
        cq, sets[3].mine = tie(cq, sets[3].mine)
        sets[3].between_cores()
    cmixed, cprobs = cross_forward(rows, cq, ck, cv, length)
    if fast:
        cmixed, sets[3].other, sets[2].other = tie(cmixed, sets[3].other, sets[2].other)
        single.finish(full)
        sets[2].finish(full)
        sets[3].finish(full)
    hidden2 = hidden + mm(cmixed, full[12], 1, 0)
    fnorm = lowered(hidden2 * norm_factor(hidden2) * fg)
    upper = mm(fnorm, full[14], 1, 0)
    active = lowered(jax.nn.gelu(upper))
    result = lowered(hidden2 + mm(active, full[15], 1, 0))

    gy = out_grad.reshape(count, width)
    g_down = lowered(mm(active, gy, 0, 0))
    if fast:
        r_down = Reduce(place, "down", [g_down], [local[15].shape])
        gy, r_down.send, result = tie(gy, r_down.send, result)
    g_active = mm(gy, full[15], 1, 1)
    g_upper = lowered(jax.vjp(jax.nn.gelu, upper)[1](g_active)[0])
    g_up = lowered(mm(fnorm, g_upper, 0, 0))
    if fast:
        r_down.between_cores()
        r_up = Reduce(place, "up", [g_up], [local[14].shape])
        g_upper, r_up.send, r_down.sums = tie(g_upper, r_up.send, r_down.sums)
    g_fnorm = mm(g_upper, full[14], 1, 1)
    part, g_fg = norm_back(hidden2, fg, g_fnorm)
    g_h2 = gy.astype(F32) + part
    g_branch = lowered(g_h2)
    g_cproj = lowered(mm(cmixed, g_branch, 0, 0))
    g_cmixed = lowered(mm(g_branch, full[12], 1, 1))
    if fast:
        r_up.between_cores()
        r_one = ReduceSingle(place, g_cproj)
        g_cmixed, r_up.sums, r_one.send = tie(g_cmixed, r_up.sums, r_one.send)
        r_one.between_cores()
    g_cq, g_ck, g_cv = cross_backward(rows, cq, g_cmixed, ck, cv, cprobs, length)
    if fast:
        r_down.in_plane(g_ck)
        r_up.in_plane(g_ck)
        g_cq, g_ck, g_cv, r_down.part, r_up.part = tie(g_cq, g_ck, g_cv, r_down.part, r_up.part)
        r_down.along_grp()
        r_up.along_grp()
    g_cquery_w = lowered(mm(cnorm, g_cq, 0, 0))
    g_ckey_w = lowered(mm(near, g_ck, 0, 0))
    g_cvalue_w = lowered(mm(near, g_cv, 0, 0))
    g_cnorm = mm(g_cq, full[9], 1, 1)
    part, g_cg = norm_back(hidden, cg, g_cnorm)
    g_h1 = g_h2 + part
    g_attn = lowered(g_h1)
    g_aproj = lowered(mm(mixed, g_attn, 0, 0))
    if fast:
        r_cross = Reduce(place, "four", [g_ckey_w, g_cvalue_w, g_aproj, g_cquery_w], [local[10].shape] * CHIPS)
        g_attn, r_cross.send = tie(g_attn, r_cross.send)
    g_near = lowered(mm(g_ck, full[10], 1, 1) + mm(g_cv, full[11], 1, 1)).reshape(neighbours.shape)
    g_mixed = lowered(mm(g_attn, full[7], 1, 1))
    if fast:
        r_cross.between_cores()
        g_mixed, g_near, r_cross.sums, r_one.part = tie(g_mixed, g_near, r_cross.sums, r_one.part)
        r_cross.in_plane()
        r_one.along_grp()
    g_q, g_k, g_v, g_relk, g_bc, g_bp = self_backward(query, bc, bp, key, value, rel_key, g_mixed, probs)
    if fast:
        g_q, g_k, g_v, r_down.mine, r_up.mine, r_one.mine, r_cross.part = tie(
            g_q, g_k, g_v, r_down.mine, r_up.mine, r_one.mine, r_cross.part
        )
        r_down.back_plane()
        r_up.back_plane()
        r_one.in_plane()
        r_cross.along_grp()
    g_rel_sum = lowered(jnp.sum(g_relk.astype(F32), axis=0))
    g_rel = lowered(mm(table, g_rel_sum, 0, 0))
    g_query_w = lowered(mm(normed, g_q, 0, 0))
    g_key_w = lowered(mm(normed, g_k, 0, 0))
    g_value_w = lowered(mm(normed, g_v, 0, 0))
    if fast:
        r_self = Reduce(place, "four", [g_query_w, g_key_w, g_value_w, g_rel], [local[1].shape] * CHIPS)
        g_q, g_k, g_v, r_self.send = tie(g_q, g_k, g_v, r_self.send)
        r_self.between_cores()
    g_normed = mm(g_q, full[1], 1, 1) + mm(g_k, full[2], 1, 1) + mm(g_v, full[3], 1, 1)
    part, g_ag = norm_back(x, ag, g_normed)
    grad_x = lowered(g_h1 + part)
    small = [g_ag, g_bc[0], g_bp[0], g_cg, g_fg]
    out = [None] * len(local)
    if fast:
        r_cross.back_plane()
        out[SINGLE] = r_one.finish()
        out[15] = r_down.finish()[0]
        out[14] = r_up.finish()[0]
        r_self.in_plane(out[14], out[15], grad_x)
        r_self.along_grp()
        r_self.back_plane()
        vectors = reduce_vectors(place, jnp.stack(small))
        for n, i in enumerate(VECTORS):
            out[i] = vectors[n]
        for i, w in zip((10, 11, 7, 9), r_cross.finish()):
            out[i] = w
        for i, w in zip((1, 2, 3, 6), r_self.finish()):
            out[i] = w
    else:
        grads = [None, g_query_w, g_key_w, g_value_w, None, None, g_rel, g_aproj, None, g_cquery_w, g_ckey_w,
                 g_cvalue_w, g_cproj, None, g_up, g_down]
        for n, i in enumerate(VECTORS):
            grads[i] = small[n]
        for i, g in enumerate(grads):
            shard = lax.psum_scatter(lowered(g), "grp", scatter_dimension=0, tiled=True)
            out[i] = lax.psum(shard.astype(F32), "rep")
    return (result.reshape(tokens.shape), grad_x.reshape(tokens.shape), g_near) + tuple(out)


def solution(mesh):
    data3 = P(("rep", "grp"), None, None)
    data2 = P(("rep", "grp"), None)
    ranks = (1, 2, 2, 2, 1, 1, 2, 2, 1, 2, 2, 2, 2, 1, 2, 2)
    weights = tuple(P("grp") if r == 1 else P("grp", None) for r in ranks)
    return jax.shard_map(
        partial(per_device, (mesh.shape["rep"], mesh.shape["grp"])),
        mesh=mesh,
        in_specs=(data3, data2, data3, data2, data3) + weights,
        out_specs=(data3, data3, data3) + weights,
        check_vma=False,
    )
```
